256 devices in a mesh: section: 4 (over y_lo, core), dp: 8 (over z), mp: 8 (over y_hi, x).
Axes of the slice: x: 4, y: 4 (y_hi: 2, y_lo: 2; y = y_hi * 2 + y_lo), z: 8, core: 2. Of those that a mesh axis runs over, the one named last changes fastest.
Arguments:
- encoder_rows: bfloat16 [96, 256, 4096], P(('section', 'dp')), may hold values from -6 to 6
- w_key: bfloat16 [4096, 4096], P(('section', 'dp'), 'mp'), may hold values from -0.09375 to 0.09375
- w_value: bfloat16 [4096, 4096], P(('section', 'dp'), 'mp'), may hold values from -0.09375 to 0.09375
- query: bfloat16 [128, 128, 4096], P(('section', 'dp'), None, 'mp'), may hold values from -80 to 80
- grad_context: bfloat16 [128, 128, 4096], P(('section', 'dp'), None, 'mp'), may hold values from -6 to 6
- source: int32 [128], replicated, may hold values from 0 to 95, as said below
Outputs:
- context: bfloat16 [128, 128, 4096], P(('section', 'dp'), None, 'mp')
- grad_query: bfloat16 [128, 128, 4096], P(('section', 'dp'), None, 'mp')
- grad_kv_weights: float32 [2, 4096, 4096], P(None, ('section', 'dp'), 'mp')
The draws below stay inside these ranges and needn't reach their ends.
Inputs may be any that keep to these rules, and one draw needn't show every extreme that they name: `source`: the sequences of one section index (the 32 consecutive sequences held at that section index) read only examples held at the same section index; the 4 sequences of one device read examples held at 4 different dp indices.
All inputs are finite; a program needn't handle non-finite values.
Results may differ from the reference program's by a relative error of at most 0.025.
The reference program's roundings to bfloat16 on the way (of `keys`, `values`, `probs`, `score_grads`, `key_terms`, `value_terms`, `grad_keys` and `grad_values`) count: a program that leaves them out, or rounds other values in their place, can miss the bound.
Values may be sent and summed in bfloat16 or wider, within the bound.
A program may use at most 128 MiB of HBM per device.

```python
import jax
import jax.numpy as jnp
from jax import lax

D = 4096
HEADS = 64
HEAD_DIM = 64
S = 256
TQ = 128
DSEQ = 4
EX_DEV = 3
EXAMPLES = 96
DEC_SEQS = 128
INNER = 4096
N_SECTION = 4
N_DP = 8


def draw_query(key, part):
    shape = (DEC_SEQS, TQ, HEADS * HEAD_DIM)
    return (0.15 * jax.random.truncated_normal(key, -6.0, 6.0, shape, jnp.float32)).astype(jnp.bfloat16)


def draw_source(key, part):
    groups = N_SECTION * N_DP
    split_keys = jax.random.split(jax.random.fold_in(key, 11), groups)
    owners = jax.vmap(lambda one: jax.random.permutation(one, N_DP))(split_keys)[:, :DSEQ]
    local = jax.random.randint(jax.random.fold_in(key, 12), (groups, DSEQ), 0, EX_DEV)
    section_of = (jnp.arange(groups, dtype=jnp.int32) // N_DP)[:, None]
    holder = section_of * N_DP + owners.astype(jnp.int32)
    return (holder * EX_DEV + local).reshape(-1).astype(jnp.int32)


def strengthened(result, key, source, target, parts, factor):
    owner, partner = [(jnp.arange(result.shape[axis_at]) // (result.shape[axis_at] // parts)).reshape([-1 if axis == axis_at else 1 for axis in range(result.ndim)]) for axis_at in (source, target)]
    chosen = jax.random.permutation(key, parts)[partner]
    strong = (owner == chosen) | (owner == (partner + parts // 2) % parts)
    return jnp.where(strong, factor * result, result)


def shard_levels(stream_key, extent, cuts, smallest, high):
    factor_of = 1.0
    for dim, blocks in cuts:
        heights = jax.random.uniform(jax.random.fold_in(jax.random.fold_in(stream_key, 6), dim), (blocks,), jnp.float32, smallest / len(cuts), high / len(cuts))
        factor_of = factor_of * jnp.repeat(jnp.exp(heights), extent[dim] // blocks).reshape((-1,) + (1,) * (len(extent) - 1 - dim))
    return factor_of


def bell_draw(rng, dims, scale, most, shards=(), kind=jnp.bfloat16):
    factor_of = shard_levels(rng, dims, shards, -0.22, 0.18) if shards else 1.0
    drawn = jax.random.normal(rng, dims, jnp.float32) * scale * factor_of
    return jnp.minimum(jnp.maximum(drawn, -most), most).astype(kind)


def heavy_noise(rng, extent, spread, reach, cuts, heavy, kind=jnp.bfloat16):
    values = spread * jax.random.normal(rng, extent, jnp.float32)
    if cuts:
        values = values * shard_levels(rng, extent, cuts, -0.22, 0.18)
    return jnp.clip(strengthened(values, jax.random.fold_in(rng, 3), *heavy), -reach, reach).astype(kind)


def setup_inputs(seed: int = 0) -> dict:
    key_of = jax.random.split(jax.random.key(seed), 7)
    return {
        "encoder_rows": heavy_noise(key_of[0], (EXAMPLES, S, D), 1.0, 6.0, ((0, 32),), (0, 2, 32, 2.75)),
        "w_key": bell_draw(key_of[1], (D, INNER), D ** -0.5, 0.09375, ((0, 32), (1, 8))),
        "w_value": bell_draw(key_of[2], (D, INNER), D ** -0.5, 0.09375, ((0, 32), (1, 8))),
        "query": draw_query(jax.random.fold_in(key_of[6], 71), 0),
        "grad_context": bell_draw(key_of[4], (DEC_SEQS, TQ, INNER), 1.0, 6.0, ((0, 32), (2, 8))),
        "source": draw_source(jax.random.fold_in(key_of[6], 71), 0),
    }


def attend(query_rows, key_rows, value_rows, grad_rows):
    qf = query_rows.astype(jnp.float32).reshape(TQ, HEADS, HEAD_DIM)
    kf = key_rows.astype(jnp.float32).reshape(S, HEADS, HEAD_DIM)
    vf = value_rows.astype(jnp.float32).reshape(S, HEADS, HEAD_DIM)
    gf = grad_rows.astype(jnp.float32).reshape(TQ, HEADS, HEAD_DIM)
    scores = jnp.einsum('thc,uhc->htu', qf, kf)
    top = jnp.max(scores, axis=-1, keepdims=True)
    expo = jnp.exp(scores - top)
    weights = expo / jnp.sum(expo, axis=-1, keepdims=True)
    probs = weights.astype(jnp.bfloat16)
    pf = probs.astype(jnp.float32)
    context = jnp.einsum('htu,uhc->thc', pf, vf).astype(jnp.bfloat16)
    dprobs = jnp.einsum('thc,uhc->htu', gf, vf)
    delta = jnp.sum(weights * dprobs, axis=-1, keepdims=True)
    score_grads = (weights * (dprobs - delta)).astype(jnp.bfloat16)
    sf = score_grads.astype(jnp.float32)
    grad_query = jnp.einsum('htu,uhc->thc', sf, kf).astype(jnp.bfloat16)
    key_terms = jnp.einsum('htu,thc->uhc', sf, qf).astype(jnp.bfloat16)
    value_terms = jnp.einsum('htu,thc->uhc', pf, gf).astype(jnp.bfloat16)
    inner = HEADS * HEAD_DIM
    return (context.reshape(TQ, inner), grad_query.reshape(TQ, inner),
            key_terms.reshape(S, inner), value_terms.reshape(S, inner))


def reference(encoder_rows, w_key, w_value, query, grad_context, source):
    inner = HEADS * HEAD_DIM
    flat = encoder_rows.reshape(EXAMPLES * S, D)
    keys = jnp.dot(flat, w_key, preferred_element_type=jnp.float32).astype(jnp.bfloat16).reshape(EXAMPLES, S, inner)
    values = jnp.dot(flat, w_value, preferred_element_type=jnp.float32).astype(jnp.bfloat16).reshape(EXAMPLES, S, inner)

    def one_sequence(index):
        example = source[index]
        key_rows = lax.dynamic_index_in_dim(keys, example, 0, keepdims=False)
        value_rows = lax.dynamic_index_in_dim(values, example, 0, keepdims=False)
        return attend(query[index], key_rows, value_rows, grad_context[index])

    context, grad_query, key_terms, value_terms = lax.map(one_sequence, jnp.arange(DEC_SEQS, dtype=jnp.int32))
    grad_keys = jax.ops.segment_sum(key_terms.astype(jnp.float32), source, num_segments=EXAMPLES).astype(jnp.bfloat16)
    grad_values = jax.ops.segment_sum(value_terms.astype(jnp.float32), source, num_segments=EXAMPLES).astype(jnp.bfloat16)
    groups = N_SECTION * N_DP
    flat_groups = flat.reshape(groups, EX_DEV * S, D)
    key_groups = grad_keys.reshape(groups, EX_DEV * S, inner)
    value_groups = grad_values.reshape(groups, EX_DEV * S, inner)

    def accumulate(totals, pieces):
        rows, key_part, value_part = pieces
        term_key = jnp.dot(rows.T, key_part, preferred_element_type=jnp.float32).astype(jnp.bfloat16)
        term_value = jnp.dot(rows.T, value_part, preferred_element_type=jnp.float32).astype(jnp.bfloat16)
        term_key, term_value = lax.optimization_barrier((term_key, term_value))
        return (totals[0] + term_key.astype(jnp.float32), totals[1] + term_value.astype(jnp.float32)), None

    start = (jnp.zeros((D, inner), jnp.float32), jnp.zeros((D, inner), jnp.float32))
    totals, unused = lax.scan(accumulate, start, (flat_groups, key_groups, value_groups))
    return context, grad_query, jnp.stack([totals[0], totals[1]], axis=0)
```

```python
import functools

import jax
import jax.numpy as jnp
from jax import lax
from jax.experimental import pallas as pl
from jax.experimental.pallas import tpu as pltpu
from jax.sharding import PartitionSpec as P

HEAD_DIM = 64
MESH = pl.DeviceIdType.MESH
BF16 = jnp.bfloat16
F32 = jnp.float32
N_DP = 8
N_MP = 8
DSEQ = 4
CHUNKS = 4
CROWS = 64
SLICE = 512
WROWS = 128
WCOLS = 1024


def gather_kernel(holder_ref, w_ref, snd_ref, wf_ref, ef_ref, *scratch):
    slots, picks = scratch[0:CHUNKS], scratch[CHUNKS : 2 * CHUNKS]
    ssem, rsem, lsem = scratch[2 * CHUNKS :]
    s, d, m = lax.axis_index("section"), lax.axis_index("dp"), lax.axis_index("mp")
    sib, ypart = (s ^ 1, d, m), (s ^ 2, d, m)
    zr, zl = (s, (d + 1) % 8, m), (s, (d + 7) % 8, m)
    x, yhi = m % 4, m // 4
    xr, xl, y2 = (s, d, yhi * 4 + (x + 1) % 4), (s, d, yhi * 4 + (x + 3) % 4), (s, d, m ^ 4)

    barrier = pltpu.get_barrier_semaphore()
    peers = [sib, ypart, xr, xl, y2] + [(s, (d + k) % 8, m) for k in range(1, 8)]
    for peer in peers:
        pl.semaphore_signal(barrier, inc=1, device_id=peer, device_id_type=MESH)
    pl.semaphore_wait(barrier, len(peers))

    count = [0]
    sent = []
    local = []

    def put(src, dst, to):
        i = count[0]
        count[0] += 1
        copy = pltpu.make_async_remote_copy(
            src_ref=src, dst_ref=dst, send_sem=ssem.at[i], recv_sem=rsem.at[i],
            device_id=to, device_id_type=MESH,
        )
        copy.start()
        sent.append(copy)
        return copy

    def keep(src, dst):
        copy = pltpu.make_async_copy(src, dst, lsem.at[len(local)])
        copy.start()
        local.append(copy)
        return copy

    def wblk(sec, k):
        return wf_ref.at[sec * 8 + (d + k + 8) % 8]

    own_w = wblk(s, 0)
    w_sib = put(w_ref, own_w, sib)
    w_yp = put(w_ref, own_w, ypart)
    keep(w_ref, own_w)
    order = (4, 3, 5, 2, 6, 1, 7)
    arrive = [None] * CHUNKS
    own_slot = [None] * CHUNKS
    wz = {}
    for c in range(CHUNKS):
        rows = pl.ds(c * CROWS, CROWS)
        own_slot[c] = keep(snd_ref.at[d, rows], slots[c].at[d])
        arrive[c] = [
            put(snd_ref.at[(d + k) % 8, rows], slots[c].at[d], (s, (d + k) % 8, m)) for k in order
        ]
        if c == 1:
            wz[1] = put(w_ref, own_w, zr)
            wz[-1] = put(w_ref, own_w, zl)
    w_yp.wait_recv()
    sib_recv = [w_sib]
    sp = s ^ 2
    sib_recv.append(put(wblk(sp, 0), wblk(sp, 0), sib))
    wp = {1: put(wblk(sp, 0), wblk(sp, 0), zr), -1: put(wblk(sp, 0), wblk(sp, 0), zl)}
    yrecv = {}

    def e_blk(mm, c):
        return ef_ref.at[mm, c]

    first = [None] * CHUNKS
    second = [None] * CHUNKS
    third = [None] * CHUNKS
    row0 = yhi * 4
    m_r, m_l, m_2 = row0 + (x + 1) % 4, row0 + (x + 3) % 4, row0 + (x + 2) % 4
    half = DSEQ * CROWS // 2

    def stage1(c):
        own_slot[c].wait()
        for copy in arrive[c]:
            copy.wait_recv()
        for n in range(DSEQ):
            picks[c][pl.ds(n * CROWS, CROWS), :] = slots[c][holder_ref[n]]
        mine = e_blk(m, c)
        first[c] = (put(picks[c], mine, xr), put(picks[c], mine, xl), put(picks[c], mine, y2))
        keep(picks[c], mine)

    def stage2(c):
        to_r, to_l, to_y = first[c]
        to_r.wait_recv()
        lo = e_blk(m_l, c).at[pl.ds(0, half)]
        a = put(lo, lo, xr)
        to_l.wait_recv()
        hi = e_blk(m_r, c).at[pl.ds(half, half)]
        b = put(hi, hi, xl)
        to_y.wait_recv()
        part = e_blk(m ^ 4, c)
        second[c] = (a, b, put(part, part, xr), put(part, part, xl))

    def stage3(c):
        second[c][0].wait_recv()
        second[c][1].wait_recv()
        far = e_blk(m_2, c)
        third[c] = put(far, far, y2)

    def w_step(j):
        wz[j].wait_recv()
        right_src = wblk(s, -j)
        if j < 3:
            wz[j + 1] = put(right_src, right_src, zr)
        else:
            lo = right_src.at[pl.ds(0, WROWS // 2)]
            wz[4] = put(lo, lo, zr)
        wz[-j].wait_recv()
        left_src = wblk(s, j)
        if j < 3:
            wz[-j - 1] = put(left_src, left_src, zl)
        else:
            hi = left_src.at[pl.ds(WROWS // 2, WROWS // 2)]
            wz[-4] = put(hi, hi, zl)
        sib_recv.append(put(right_src, right_src, sib))
        sib_recv.append(put(left_src, left_src, sib))
        if j >= 2:
            yrecv[j] = put(right_src, right_src, ypart)
            yrecv[-j] = put(left_src, left_src, ypart)

    stage1(0)
    stage1(1)
    stage2(0)
    w_step(1)
    stage1(2)
    stage2(1)
    stage3(0)
    stage1(3)
    w_step(2)
    stage2(2)
    stage3(1)
    w_step(3)
    stage2(3)
    stage3(2)
    wz[4].wait_recv()
    wz[-4].wait_recv()
    far_w = wblk(s, 4)
    sib_recv.append(put(far_w, far_w, sib))
    yrecv[4] = put(far_w, far_w, ypart)
    for j in (1, -1):
        wp[j].wait_recv()
        blk = wblk(sp, -j)
        sib_recv.append(put(blk, blk, sib))
    stage3(3)
    for j in (2, -2, 3, -3, 4):
        yrecv[j].wait_recv()
        blk = wblk(sp, -j)
        sib_recv.append(put(blk, blk, sib))
    for c in range(CHUNKS):
        second[c][2].wait_recv()
        second[c][3].wait_recv()
        third[c].wait_recv()
    for copy in sib_recv:
        copy.wait_recv()
    for copy in sent:
        copy.wait_send()
    for copy in local:
        if not any(copy is other for other in own_slot):
            copy.wait()


def gather(holder, w_cat, enc_send):
    n_copies = 32 + 28 + 8 * CHUNKS
    any_spec = pl.BlockSpec(memory_space=pl.ANY)
    return pl.pallas_call(
        gather_kernel,
        out_shape=(
            jax.ShapeDtypeStruct((32, WROWS, WCOLS), BF16),
            jax.ShapeDtypeStruct((N_MP, CHUNKS, DSEQ * CROWS, SLICE), BF16),
        ),
        in_specs=[
            pl.BlockSpec(memory_space=pltpu.SMEM),
            pl.BlockSpec(memory_space=pltpu.VMEM),
            any_spec,
        ],
        out_specs=(any_spec, any_spec),
        scratch_shapes=[pltpu.VMEM((N_DP, CROWS, SLICE), BF16)] * CHUNKS
        + [pltpu.VMEM((DSEQ * CROWS, SLICE), BF16)] * CHUNKS
        + [
            pltpu.SemaphoreType.DMA((n_copies,)),
            pltpu.SemaphoreType.DMA((n_copies,)),
            pltpu.SemaphoreType.DMA((1 + 2 * CHUNKS,)),
        ],
        compiler_params=pltpu.CompilerParams(collective_id=0, has_side_effects=True),
        name="gather_rows",
    )(holder, w_cat, enc_send)


def project_kernel(e_ref, w_ref, o_ref, acc):
    i = pl.program_id(0)
    term = jnp.dot(e_ref[0], w_ref[0], preferred_element_type=F32)

    @pl.when(i == 0)
    def _():
        acc[...] = term

    @pl.when(i > 0)
    def _():
        acc[...] += term

    @pl.when(i == pl.num_programs(0) - 1)
    def _():
        o_ref[...] = acc[...].astype(BF16)


def project(enc, w):
    rows = enc.shape[1]
    return pl.pallas_call(
        project_kernel,
        grid=(N_MP,),
        out_shape=jax.ShapeDtypeStruct((rows, WCOLS), BF16),
        in_specs=[
            pl.BlockSpec((1, rows, SLICE), lambda i: (i, 0, 0)),
            pl.BlockSpec((1, SLICE, WCOLS), lambda i: (i, 0, 0)),
        ],
        out_specs=pl.BlockSpec((rows, WCOLS), lambda i: (0, 0)),
        scratch_shapes=[pltpu.VMEM((rows, WCOLS), F32)],
        name="project",
    )(enc, w)


def nt(a, b):
    return lax.dot_general(a, b, (((1,), (1,)), ((), ())), preferred_element_type=F32)


def nn(a, b):
    return lax.dot_general(a, b, (((1,), (0,)), ((), ())), preferred_element_type=F32)


def tn(a, b):
    return lax.dot_general(a, b, (((0,), (0,)), ((), ())), preferred_element_type=F32)


def attend_kernel(k_ref, v_ref, q_ref, g_ref, ctx_ref, gq_ref, kt_ref, vt_ref):
    seq = CHUNKS * CROWS
    k = k_ref[...].reshape(seq, 128)
    v = v_ref[...].reshape(seq, 128)
    q, g = q_ref[0], g_ref[0]
    rows = q.shape[0]
    low = lax.broadcasted_iota(jnp.int32, q.shape, 1) < HEAD_DIM
    zero = jnp.zeros_like(q)
    q2 = jnp.concatenate([jnp.where(low, q, zero), jnp.where(low, zero, q)], axis=0)
    g2 = jnp.concatenate([jnp.where(low, g, zero), jnp.where(low, zero, g)], axis=0)
    scores = nt(q2, k)
    top = jnp.max(scores, axis=-1, keepdims=True)
    expo = jnp.exp(scores - top)
    weights = expo / jnp.sum(expo, axis=-1, keepdims=True)
    probs = weights.astype(BF16)
    dprobs = nt(g2, v)
    delta = jnp.sum(weights * dprobs, axis=-1, keepdims=True)
    grads = (weights * (dprobs - delta)).astype(BF16)
    ctx = nn(probs, v)
    gq = nn(grads, k)
    ctx_ref[0] = jnp.where(low, ctx[:rows], ctx[rows:]).astype(BF16)
    gq_ref[0] = jnp.where(low, gq[:rows], gq[rows:]).astype(BF16)
    kt_ref[...] = tn(grads, q2).astype(BF16).reshape(kt_ref.shape)
    vt_ref[...] = tn(probs, g2).astype(BF16).reshape(vt_ref.shape)


def attend(kv, query, grad_context):
    q_rows, inner = query.shape[1:]
    pairs = inner // 128
    k_spec = pl.BlockSpec((CHUNKS, 1, CROWS, 128), lambda n, h: (0, n, 0, h))
    v_spec = pl.BlockSpec((CHUNKS, 1, CROWS, 128), lambda n, h: (0, n, 0, h + pairs))
    q_spec = pl.BlockSpec((1, q_rows, 128), lambda n, h: (n, 0, h))
    kv4 = kv.reshape(CHUNKS, DSEQ, CROWS, WCOLS)
    half = jax.ShapeDtypeStruct((CHUNKS, DSEQ, CROWS, inner), BF16)
    return pl.pallas_call(
        attend_kernel,
        grid=(DSEQ, pairs),
        out_shape=(
            jax.ShapeDtypeStruct(query.shape, BF16),
            jax.ShapeDtypeStruct(query.shape, BF16),
            half,
            half,
        ),
        in_specs=[k_spec, v_spec, q_spec, q_spec],
        out_specs=(q_spec, q_spec, k_spec, k_spec),
        name="attend",
    )(kv4, kv4, query, grad_context)


def weight_grad_kernel(e_ref, k_ref, v_ref, o_ref):
    e = e_ref[0]
    inner = k_ref.shape[1]
    o_ref[:, :inner] = tn(e, k_ref[...]).astype(BF16)
    o_ref[:, inner:] = tn(e, v_ref[...]).astype(BF16)


def weight_grad(enc, key_terms, value_terms):
    rows, inner = key_terms.shape
    return pl.pallas_call(
        weight_grad_kernel,
        grid=(N_MP,),
        out_shape=jax.ShapeDtypeStruct((N_MP * SLICE, WCOLS), BF16),
        in_specs=[
            pl.BlockSpec((1, rows, SLICE), lambda i: (i, 0, 0)),
            pl.BlockSpec((rows, inner), lambda i: (0, 0)),
            pl.BlockSpec((rows, inner), lambda i: (0, 0)),
        ],
        out_specs=pl.BlockSpec((SLICE, WCOLS), lambda i: (i, 0)),
        name="weight_grad",
    )(enc, key_terms, value_terms)


def per_device(encoder_rows, w_key, w_value, query, grad_context, source):
    ex_dev = encoder_rows.shape[0]
    dec_dev, q_rows, inner = query.shape
    s, d, m = lax.axis_index("section"), lax.axis_index("dp"), lax.axis_index("mp")
    per_section = N_DP * dec_dev
    plan = lax.dynamic_slice_in_dim(source, s * per_section, per_section).reshape(N_DP, dec_dev)
    holder_dp = plan // ex_dev - s * N_DP
    local_ex = plan % ex_dev
    chosen = jnp.sum(jnp.where(holder_dp == d, local_ex, 0), axis=1)
    my_holder = lax.dynamic_index_in_dim(holder_dp, d, 0, keepdims=False)
    columns = lax.dynamic_slice_in_dim(encoder_rows, m * SLICE, SLICE, axis=2)
    enc_send = jnp.take(columns, chosen, axis=0, mode="clip")
    w_cat = jnp.concatenate([w_key, w_value], axis=1)
    w_full, enc_full = gather(my_holder, w_cat, enc_send)
    enc = enc_full.reshape(N_MP, DSEQ * CHUNKS * CROWS, SLICE)
    kv = project(enc, w_full.reshape(N_MP, SLICE, WCOLS))
    context, grad_query, key_terms, value_terms = attend(kv, query, grad_context)
    part = weight_grad(enc, key_terms.reshape(-1, inner), value_terms.reshape(-1, inner))
    grad_rows = lax.psum_scatter(
        part, ("section", "dp"), scatter_dimension=0, tiled=True
    ).astype(F32)
    grad_kv_weights = jnp.stack([grad_rows[:, :inner], grad_rows[:, inner:]], axis=0)
    return context, grad_query, grad_kv_weights


def solution(mesh):
    return jax.shard_map(
        per_device,
        mesh=mesh,
        in_specs=(
            P(("section", "dp"), None, None),
            P(("section", "dp"), "mp"),
            P(("section", "dp"), "mp"),
            P(("section", "dp"), None, "mp"),
            P(("section", "dp"), None, "mp"),
            P(),
        ),
        out_specs=(
            P(("section", "dp"), None, "mp"),
            P(("section", "dp"), None, "mp"),
            P(None, ("section", "dp"), "mp"),
        ),
        check_vma=False,
    )
```

```python
import functools

import jax
import jax.numpy as jnp
from jax import lax
from jax.experimental import pallas as pl
from jax.experimental.pallas import tpu as pltpu
from jax.sharding import PartitionSpec as P

HEAD_DIM = 64
MESH = pl.DeviceIdType.MESH
BF16 = jnp.bfloat16
F32 = jnp.float32
N_DP = 8
N_MP = 8
DSEQ = 4
CHUNKS = 4
CROWS = 64
SLICE = 512
WROWS = 128
WCOLS = 1024


def gather_kernel(holder_ref, w_ref, snd_ref, wf_ref, ef_ref, *scratch):
    slots, picks = scratch[0:CHUNKS], scratch[CHUNKS : 2 * CHUNKS]
    ssem, rsem, lsem = scratch[2 * CHUNKS :]
    s, d, m = lax.axis_index("section"), lax.axis_index("dp"), lax.axis_index("mp")
    sib, ypart = (s ^ 1, d, m), (s ^ 2, d, m)
    zr, zl = (s, (d + 1) % 8, m), (s, (d + 7) % 8, m)
    x, yhi = m % 4, m // 4
    xr, xl, y2 = (s, d, yhi * 4 + (x + 1) % 4), (s, d, yhi * 4 + (x + 3) % 4), (s, d, m ^ 4)

    barrier = pltpu.get_barrier_semaphore()
    peers = [sib, ypart, xr, xl, y2] + [(s, (d + k) % 8, m) for k in range(1, 8)]
    for peer in peers:
        pl.semaphore_signal(barrier, inc=1, device_id=peer, device_id_type=MESH)
    pl.semaphore_wait(barrier, len(peers))

    count = [0]
    sent = []
    local = []

    def put(src, dst, to):
        i = count[0]
        count[0] += 1
        copy = pltpu.make_async_remote_copy(
            src_ref=src, dst_ref=dst, send_sem=ssem.at[i], recv_sem=rsem.at[i],
            device_id=to, device_id_type=MESH,
        )
        copy.start()
        sent.append(copy)
        return copy

    def keep(src, dst):
        copy = pltpu.make_async_copy(src, dst, lsem.at[len(local)])
        copy.start()
        local.append(copy)
        return copy

    def wblk(sec, k):
        return wf_ref.at[sec * 8 + (d + k + 8) % 8]

    own_w = wblk(s, 0)
    w_sib = put(w_ref, own_w, sib)
    w_yp = put(w_ref, own_w, ypart)
    keep(w_ref, own_w)
    order = (4, 3, 5, 2, 6, 1, 7)
    arrive = [None] * CHUNKS
    own_slot = [None] * CHUNKS
    wz = {}
    for c in range(CHUNKS):
        rows = pl.ds(c * CROWS, CROWS)
        own_slot[c] = keep(snd_ref.at[d, rows], slots[c].at[d])
        arrive[c] = [
            put(snd_ref.at[(d + k) % 8, rows], slots[c].at[d], (s, (d + k) % 8, m)) for k in order
        ]
        if c == 1:
            wz[1] = put(w_ref, own_w, zr)
            wz[-1] = put(w_ref, own_w, zl)
    w_yp.wait_recv()
    sib_recv = [w_sib]
    sp = s ^ 2
    sib_recv.append(put(wblk(sp, 0), wblk(sp, 0), sib))
    wp = {1: put(wblk(sp, 0), wblk(sp, 0), zr), -1: put(wblk(sp, 0), wblk(sp, 0), zl)}
    yrecv = {}

    def e_blk(mm, c):
        return ef_ref.at[mm, c]

    first = [None] * CHUNKS
    second = [None] * CHUNKS
    third = [None] * CHUNKS
    row0 = yhi * 4
    m_r, m_l, m_2 = row0 + (x + 1) % 4, row0 + (x + 3) % 4, row0 + (x + 2) % 4
    half = DSEQ * CROWS // 2

    def stage1(c):
        own_slot[c].wait()
        for copy in arrive[c]:
            copy.wait_recv()
        for n in range(DSEQ):
            picks[c][pl.ds(n * CROWS, CROWS), :] = slots[c][holder_ref[n]]
        mine = e_blk(m, c)
        first[c] = (put(picks[c], mine, xr), put(picks[c], mine, xl), put(picks[c], mine, y2))
        keep(picks[c], mine)

    def stage2(c):
        to_r, to_l, to_y = first[c]
        to_r.wait_recv()
        lo = e_blk(m_l, c).at[pl.ds(0, half)]
        a = put(lo, lo, xr)
        to_l.wait_recv()
        hi = e_blk(m_r, c).at[pl.ds(half, half)]
        b = put(hi, hi, xl)
        to_y.wait_recv()
        part = e_blk(m ^ 4, c)
        second[c] = (a, b, put(part, part, xr), put(part, part, xl))

    def stage3(c):
        second[c][0].wait_recv()
        second[c][1].wait_recv()
        far = e_blk(m_2, c)
        third[c] = put(far, far, y2)

    def w_step(j):
        wz[j].wait_recv()
        right_src = wblk(s, -j)
        if j < 3:
            wz[j + 1] = put(right_src, right_src, zr)
        else:
            lo = right_src.at[pl.ds(0, WROWS // 2)]
            wz[4] = put(lo, lo, zr)
        wz[-j].wait_recv()
        left_src = wblk(s, j)
        if j < 3:
            wz[-j - 1] = put(left_src, left_src, zl)
        else:
            hi = left_src.at[pl.ds(WROWS // 2, WROWS // 2)]
            wz[-4] = put(hi, hi, zl)
        sib_recv.append(put(right_src, right_src, sib))
        sib_recv.append(put(left_src, left_src, sib))
        if j >= 2:
            yrecv[j] = put(right_src, right_src, ypart)
            yrecv[-j] = put(left_src, left_src, ypart)

    stage1(0)
    stage1(1)
    stage2(0)
    w_step(1)
    stage1(2)
    stage2(1)
    stage3(0)
    stage1(3)
    w_step(2)
    stage2(2)
    stage3(1)
    w_step(3)
    stage2(3)
    stage3(2)
    wz[4].wait_recv()
    wz[-4].wait_recv()
    far_w = wblk(s, 4)
    sib_recv.append(put(far_w, far_w, sib))
    yrecv[4] = put(far_w, far_w, ypart)
    for j in (1, -1):
        wp[j].wait_recv()
        blk = wblk(sp, -j)
        sib_recv.append(put(blk, blk, sib))
    stage3(3)
    for j in (2, -2, 3, -3, 4):
        yrecv[j].wait_recv()
        blk = wblk(sp, -j)
        sib_recv.append(put(blk, blk, sib))
    for c in range(CHUNKS):
        second[c][2].wait_recv()
        second[c][3].wait_recv()
        third[c].wait_recv()
    for copy in sib_recv:
        copy.wait_recv()
    for copy in sent:
        copy.wait_send()
    for copy in local:
        if not any(copy is other for other in own_slot):
            copy.wait()


def gather(holder, w_cat, enc_send):
    n_copies = 32 + 28 + 8 * CHUNKS
    any_spec = pl.BlockSpec(memory_space=pl.ANY)
    return pl.pallas_call(
        gather_kernel,
        out_shape=(
            jax.ShapeDtypeStruct((32, WROWS, WCOLS), BF16),
            jax.ShapeDtypeStruct((N_MP, CHUNKS, DSEQ * CROWS, SLICE), BF16),
        ),
        in_specs=[
            pl.BlockSpec(memory_space=pltpu.SMEM),
            pl.BlockSpec(memory_space=pltpu.VMEM),
            any_spec,
        ],
        out_specs=(any_spec, any_spec),
        scratch_shapes=[pltpu.VMEM((N_DP, CROWS, SLICE), BF16)] * CHUNKS
        + [pltpu.VMEM((DSEQ * CROWS, SLICE), BF16)] * CHUNKS
        + [
            pltpu.SemaphoreType.DMA((n_copies,)),
            pltpu.SemaphoreType.DMA((n_copies,)),
            pltpu.SemaphoreType.DMA((1 + 2 * CHUNKS,)),
        ],
        compiler_params=pltpu.CompilerParams(collective_id=0, has_side_effects=True),
        name="gather_rows",
    )(holder, w_cat, enc_send)


def project_kernel(e_ref, w_ref, o_ref, acc):
    i = pl.program_id(0)
    term = jnp.dot(e_ref[0], w_ref[0], preferred_element_type=F32)

    @pl.when(i == 0)
    def _():
        acc[...] = term

    @pl.when(i > 0)
    def _():
        acc[...] += term

    @pl.when(i == pl.num_programs(0) - 1)
    def _():
        o_ref[...] = acc[...].astype(BF16)


def project(enc, w):
    rows = enc.shape[1]
    return pl.pallas_call(
        project_kernel,
        grid=(N_MP,),
        out_shape=jax.ShapeDtypeStruct((rows, WCOLS), BF16),
        in_specs=[
            pl.BlockSpec((1, rows, SLICE), lambda i: (i, 0, 0)),
            pl.BlockSpec((1, SLICE, WCOLS), lambda i: (i, 0, 0)),
        ],
        out_specs=pl.BlockSpec((rows, WCOLS), lambda i: (0, 0)),
        scratch_shapes=[pltpu.VMEM((rows, WCOLS), F32)],
        name="project",
    )(enc, w)


def nt(a, b):
    return lax.dot_general(a, b, (((1,), (1,)), ((), ())), preferred_element_type=F32)


def nn(a, b):
    return lax.dot_general(a, b, (((1,), (0,)), ((), ())), preferred_element_type=F32)


def tn(a, b):
    return lax.dot_general(a, b, (((0,), (0,)), ((), ())), preferred_element_type=F32)


def attend_kernel(k_ref, v_ref, q_ref, g_ref, ctx_ref, gq_ref, kt_ref, vt_ref):
    seq = CHUNKS * CROWS
    k = k_ref[...].reshape(seq, 128)
    v = v_ref[...].reshape(seq, 128)
    q, g = q_ref[0], g_ref[0]
    rows = q.shape[0]
    low = lax.broadcasted_iota(jnp.int32, q.shape, 1) < HEAD_DIM
    zero = jnp.zeros_like(q)
    q2 = jnp.concatenate([jnp.where(low, q, zero), jnp.where(low, zero, q)], axis=0)
    g2 = jnp.concatenate([jnp.where(low, g, zero), jnp.where(low, zero, g)], axis=0)
    scores = nt(q2, k)
    top = jnp.max(scores, axis=-1, keepdims=True)
    expo = jnp.exp(scores - top)
    weights = expo / jnp.sum(expo, axis=-1, keepdims=True)
    probs = weights.astype(BF16)
    dprobs = nt(g2, v)
    delta = jnp.sum(weights * dprobs, axis=-1, keepdims=True)
    grads = (weights * (dprobs - delta)).astype(BF16)
    ctx = nn(probs, v)
    gq = nn(grads, k)
    ctx_ref[0] = jnp.where(low, ctx[:rows], ctx[rows:]).astype(BF16)
    gq_ref[0] = jnp.where(low, gq[:rows], gq[rows:]).astype(BF16)
    kt_ref[...] = tn(grads, q2).astype(BF16).reshape(kt_ref.shape)
    vt_ref[...] = tn(probs, g2).astype(BF16).reshape(vt_ref.shape)


def attend(kv, query, grad_context):
    q_rows, inner = query.shape[1:]
    pairs = inner // 128
    k_spec = pl.BlockSpec((CHUNKS, 1, CROWS, 128), lambda n, h: (0, n, 0, h))
    v_spec = pl.BlockSpec((CHUNKS, 1, CROWS, 128), lambda n, h: (0, n, 0, h + pairs))
    q_spec = pl.BlockSpec((1, q_rows, 128), lambda n, h: (n, 0, h))
    kv4 = kv.reshape(CHUNKS, DSEQ, CROWS, WCOLS)
    half = jax.ShapeDtypeStruct((CHUNKS, DSEQ, CROWS, inner), BF16)
    return pl.pallas_call(
        attend_kernel,
        grid=(DSEQ, pairs),
        out_shape=(
            jax.ShapeDtypeStruct(query.shape, BF16),
            jax.ShapeDtypeStruct(query.shape, BF16),
            half,
            half,
        ),
        in_specs=[k_spec, v_spec, q_spec, q_spec],
        out_specs=(q_spec, q_spec, k_spec, k_spec),
        name="attend",
    )(kv4, kv4, query, grad_context)


def reduce_kernel(e_hbm, k_ref, v_ref, o_ref, e_ref, tosib, fromsib, own, ysend, yrecv, psend, precv,
                  zsend, zrecv, lsem, sib_s, sib_r, y_s, y_r, p_s, p_r, z_s, z_r):
    s, d, m = lax.axis_index("section"), lax.axis_index("dp"), lax.axis_index("mp")
    core, ylo = s % 2, s // 2
    sib, ypart = (s ^ 1, d, m), (s ^ 2, d, m)
    zr, zl = (s, (d + 1) % 8, m), (s, (d + 7) % 8, m)
    loads = [pltpu.make_async_copy(e_hbm.at[i], e_ref.at[i], lsem.at[i]) for i in range(N_MP)]
    for copy in loads:
        copy.start()
    barrier = pltpu.get_barrier_semaphore()
    for peer in (sib, ypart, zr, zl):
        pl.semaphore_signal(barrier, inc=1, device_id=peer, device_id_type=MESH)
    pl.semaphore_wait(barrier, 4)
    for copy in loads:
        copy.wait()

    def remote(src, dst, ss, rs, to):
        return pltpu.make_async_remote_copy(
            src_ref=src, dst_ref=dst, send_sem=ss, recv_sem=rs, device_id=to, device_id_type=MESH
        )

    def to_sib(i):
        return remote(tosib.at[i], fromsib.at[i], sib_s.at[i], sib_r.at[i], sib)

    def to_y(k):
        return remote(ysend.at[k], yrecv.at[k], y_s.at[k], y_r.at[k], ypart)

    def to_p(k):
        return remote(psend.at[k], precv.at[k], p_s.at[k], p_r.at[k], zr if k == 0 else zl)

    def to_z(k):
        to = zr if k % 2 == 0 else zl
        if k < 2:
            rows = pl.ds(k * (WROWS // 2), WROWS // 2)
            return remote(zsend.at[k, rows], zrecv.at[k, rows], z_s.at[k], z_r.at[k], to)
        return remote(zsend.at[k], zrecv.at[k], z_s.at[k], z_r.at[k], to)

    def columns(yy, cc, dd):
        block = (yy * 2 + cc) * 8 + dd
        return e_ref[block // 4, :, pl.ds(pl.multiple_of((block % 4) * WROWS, WROWS), WROWS)]

    inner = k_ref.shape[1]

    def pair(cc, dd, store):
        e = jnp.concatenate([columns(1 - ylo, cc, dd), columns(ylo, cc, dd)], axis=1)
        store(0, tn(e, k_ref[...]))
        store(inner, tn(e, v_ref[...]))

    def absorb(k):
        to_sib(k).wait_recv()
        own[k] += fromsib[k].astype(F32)

    def start_chain():
        to_y(0).wait_recv()
        total = own[0, WROWS:] + yrecv[0].astype(F32)
        half = WROWS // 2
        zsend[0, :half] = total[:half].astype(BF16)
        to_z(0).start()
        zsend[1, half:] = total[half:].astype(BF16)
        to_z(1).start()

    def step(i, carry):
        j = (i % 2) * (4 - (i + 1) // 2) + (1 - i % 2) * (4 + i // 2)
        dd = (d + j) % 8

        def store_sib(at, value):
            tosib[i, :, at : at + inner] = value.astype(BF16)

        def store_own(at, value):
            own[i, :, at : at + inner] = value

        pair(1 - core, dd, store_sib)
        to_sib(i).start()
        pair(core, dd, store_own)

        @pl.when(i == 6)
        def _():
            start_chain()

        @pl.when(i > 0)
        def _():
            absorb(i - 1)

        @pl.when((i > 0) & (i < 6))
        def _():
            ysend[i - 1] = own[i - 1, :WROWS].astype(BF16)
            to_y(i - 1).start()

        return carry

    lax.fori_loop(0, 8, step, 0)
    absorb(7)
    half = WROWS // 2
    to_y(1).wait_recv()
    total = own[1, WROWS:] + yrecv[1].astype(F32)
    to_z(0).wait_recv()
    zsend[2, :half] = (total[:half] + zrecv[0, :half].astype(F32)).astype(BF16)
    zsend[2, half:] = total[half:].astype(BF16)
    to_z(2).start()
    to_y(2).wait_recv()
    total = own[2, WROWS:] + yrecv[2].astype(F32)
    to_z(1).wait_recv()
    zsend[3, :half] = total[:half].astype(BF16)
    zsend[3, half:] = (total[half:] + zrecv[1, half:].astype(F32)).astype(BF16)
    to_z(3).start()
    for k in range(2):
        psend[k] = own[5 + k, :WROWS].astype(BF16)
        to_p(k).start()
    for k in range(2):
        to_y(3 + k).wait_recv()
        total = own[3 + k, WROWS:] + yrecv[3 + k].astype(F32)
        to_z(2 + k).wait_recv()
        zsend[4 + k] = (total + zrecv[2 + k].astype(F32)).astype(BF16)
        to_z(4 + k).start()
    total = own[7, :WROWS]
    for k in range(2):
        to_p(k).wait_recv()
        total = total + precv[k].astype(F32)
    ysend[5] = total.astype(BF16)
    to_y(5).start()
    for k in range(2):
        to_z(4 + k).wait_recv()
        zsend[6 + k] = (own[5 + k, WROWS:] + zrecv[4 + k].astype(F32)).astype(BF16)
        to_z(6 + k).start()
    total = own[7, WROWS:]
    for k in range(2):
        to_z(6 + k).wait_recv()
        total = total + zrecv[6 + k].astype(F32)
    to_y(5).wait_recv()
    total = total + yrecv[5].astype(F32)
    o_ref[0] = total[:, :inner]
    o_ref[1] = total[:, inner:]
    for k in range(8):
        to_sib(k).wait_send()
        to_z(k).wait_send()
    for k in range(6):
        to_y(k).wait_send()
    for k in range(2):
        to_p(k).wait_send()


def weight_grad(enc, key_terms, value_terms):
    rows, inner = key_terms.shape
    vmem = pl.BlockSpec(memory_space=pltpu.VMEM)
    dma = pltpu.SemaphoreType.DMA
    return pl.pallas_call(
        reduce_kernel,
        out_shape=jax.ShapeDtypeStruct((2, WROWS, inner), F32),
        in_specs=[pl.BlockSpec(memory_space=pl.ANY), vmem, vmem],
        out_specs=vmem,
        scratch_shapes=[
            pltpu.VMEM((N_MP, rows, SLICE), BF16),
            pltpu.VMEM((8, 2 * WROWS, WCOLS), BF16),
            pltpu.VMEM((8, 2 * WROWS, WCOLS), BF16),
            pltpu.VMEM((8, 2 * WROWS, WCOLS), F32),
            pltpu.VMEM((6, WROWS, WCOLS), BF16),
            pltpu.VMEM((6, WROWS, WCOLS), BF16),
            pltpu.VMEM((2, WROWS, WCOLS), BF16),
            pltpu.VMEM((2, WROWS, WCOLS), BF16),
            pltpu.VMEM((8, WROWS, WCOLS), BF16),
            pltpu.VMEM((8, WROWS, WCOLS), BF16),
            dma((N_MP,)), dma((8,)), dma((8,)), dma((6,)), dma((6,)),
            dma((2,)), dma((2,)), dma((8,)), dma((8,)),
        ],
        compiler_params=pltpu.CompilerParams(
            collective_id=1, has_side_effects=True, vmem_limit_bytes=56 * 2**20
        ),
        name="weight_grad",
    )(enc, key_terms, value_terms)


def per_device(encoder_rows, w_key, w_value, query, grad_context, source):
    ex_dev = encoder_rows.shape[0]
    dec_dev, q_rows, inner = query.shape
    s, d, m = lax.axis_index("section"), lax.axis_index("dp"), lax.axis_index("mp")
    per_section = N_DP * dec_dev
    plan = lax.dynamic_slice_in_dim(source, s * per_section, per_section).reshape(N_DP, dec_dev)
    holder_dp = plan // ex_dev - s * N_DP
    local_ex = plan % ex_dev
    chosen = jnp.sum(jnp.where(holder_dp == d, local_ex, 0), axis=1)
    my_holder = lax.dynamic_index_in_dim(holder_dp, d, 0, keepdims=False)
    columns = lax.dynamic_slice_in_dim(encoder_rows, m * SLICE, SLICE, axis=2)
    enc_send = jnp.take(columns, chosen, axis=0, mode="clip")
    w_cat = jnp.concatenate([w_key, w_value], axis=1)
    w_full, enc_full = gather(my_holder, w_cat, enc_send)
    enc = enc_full.reshape(N_MP, DSEQ * CHUNKS * CROWS, SLICE)
    kv = project(enc, w_full.reshape(N_MP, SLICE, WCOLS))
    context, grad_query, key_terms, value_terms = attend(kv, query, grad_context)
    grad_kv_weights = weight_grad(
        enc, key_terms.reshape(-1, inner), value_terms.reshape(-1, inner)
    )
    return context, grad_query, grad_kv_weights


def solution(mesh):
    return jax.shard_map(
        per_device,
        mesh=mesh,
        in_specs=(
            P(("section", "dp"), None, None),
            P(("section", "dp"), "mp"),
            P(("section", "dp"), "mp"),
            P(("section", "dp"), None, "mp"),
            P(("section", "dp"), None, "mp"),
            P(),
        ),
        out_specs=(
            P(("section", "dp"), None, "mp"),
            P(("section", "dp"), None, "mp"),
            P(None, ("section", "dp"), "mp"),
        ),
        check_vma=False,
    )
```

```python
import jax
import jax.numpy as jnp
from jax import lax
from jax.experimental import pallas as pl
from jax.experimental.pallas import tpu as pltpu
from jax.sharding import PartitionSpec as P

HEAD_DIM = 64
MESH = pl.DeviceIdType.MESH
BF16 = jnp.bfloat16
F32 = jnp.float32
N_DP = 8
N_MP = 8
DSEQ = 4
SEQ = 256
CHUNKS = 4
CROWS = SEQ // CHUNKS
SLICE = 512
WROWS = 128
HALF = 256
LANES = 128
GATHER_COPIES = (7 + 8) * CHUNKS + 2 * 18


def nt(a, b):
    return lax.dot_general(a, b, (((1,), (1,)), ((), ())), preferred_element_type=F32)


def nn(a, b):
    return lax.dot_general(a, b, (((1,), (0,)), ((), ())), preferred_element_type=F32)


def tn(a, b):
    return lax.dot_general(a, b, (((0,), (0,)), ((), ())), preferred_element_type=F32)


def attend_pair(k, v, q, g):
    rows = q.shape[0]
    low = lax.broadcasted_iota(jnp.int32, q.shape, 1) < HEAD_DIM
    zero = jnp.zeros_like(q)
    q2 = jnp.concatenate([jnp.where(low, q, zero), jnp.where(low, zero, q)], axis=0)
    g2 = jnp.concatenate([jnp.where(low, g, zero), jnp.where(low, zero, g)], axis=0)
    scores = nt(q2, k)
    top = jnp.max(scores, axis=-1, keepdims=True)
    expo = jnp.exp(scores - top)
    weights = expo / jnp.sum(expo, axis=-1, keepdims=True)
    probs = weights.astype(BF16)
    dprobs = nt(g2, v)
    delta = jnp.sum(weights * dprobs, axis=-1, keepdims=True)
    grads = (weights * (dprobs - delta)).astype(BF16)
    ctx = nn(probs, v)
    gq = nn(grads, k)
    return (
        jnp.where(low, ctx[:rows], ctx[rows:]).astype(BF16),
        jnp.where(low, gq[:rows], gq[rows:]).astype(BF16),
        tn(grads, q2).astype(BF16),
        tn(probs, g2).astype(BF16),
    )


def kernel(holder_ref, w_ref, q_ref, g_ref, snd_ref, ctx_ref, gq_ref, o_ref, *scratch):
    slots, picks = scratch[0:CHUNKS], scratch[CHUNKS : 2 * CHUNKS]
    (ef, wf, kv, terms, tosib, fromsib, own, ysend, yrecv, psend, precv, zsend, zrecv,
     ssem, rsem, lsem, sib_s, sib_r, y_s, y_r, p_s, p_r, z_s, z_r) = scratch[2 * CHUNKS :]
    s, d, m = lax.axis_index("section"), lax.axis_index("dp"), lax.axis_index("mp")
    core, ylo = s % 2, s // 2
    sib, ypart = (s ^ 1, d, m), (s ^ 2, d, m)
    zr, zl = (s, (d + 1) % 8, m), (s, (d + 7) % 8, m)
    x, yhi = m % 4, m // 4
    m_r, m_l, m_2 = yhi * 4 + (x + 1) % 4, yhi * 4 + (x + 3) % 4, yhi * 4 + (x + 2) % 4
    xr, xl, y2 = (s, d, m_r), (s, d, m_l), (s, d, m ^ 4)

    barrier = pltpu.get_barrier_semaphore()
    peers = [sib, ypart, xr, xl, y2] + [(s, (d + k) % 8, m) for k in range(1, 8)]
    for peer in peers:
        pl.semaphore_signal(barrier, inc=1, device_id=peer, device_id_type=MESH)

    sent, local = [], []

    def put(src, dst, to):
        i = len(sent)
        copy = pltpu.make_async_remote_copy(
            src_ref=src, dst_ref=dst, send_sem=ssem.at[i], recv_sem=rsem.at[i],
            device_id=to, device_id_type=MESH,
        )
        copy.start()
        sent.append(copy)
        return copy

    def keep(src, dst):
        copy = pltpu.make_async_copy(src, dst, lsem.at[len(local)])
        copy.start()
        local.append(copy)
        return copy

    order = (4, 3, 5, 2, 6, 1, 7)
    arrive, own_slot, own_pick = [None] * CHUNKS, [None] * CHUNKS, [None] * CHUNKS
    first, second, third = [None] * CHUNKS, [None] * CHUNKS, [None] * CHUNKS
    mid = DSEQ * CROWS // 2

    def rows_out(c):
        rows = pl.ds(c * CROWS, CROWS)
        arrive[c] = [
            put(snd_ref.at[(d + k) % 8, rows], slots[c].at[d], (s, (d + k) % 8, m)) for k in order
        ]

    def stage1(c):
        own_slot[c].wait()
        for copy in arrive[c]:
            copy.wait_recv()
        for n in range(DSEQ):
            picks[c][pl.ds(n * CROWS, CROWS), :] = slots[c][holder_ref[n]]
        mine = ef.at[m, c]
        first[c] = (put(picks[c], mine, xr), put(picks[c], mine, xl), put(picks[c], mine, y2))
        own_pick[c] = keep(picks[c], mine)

    def stage2(c):
        to_r, to_l, to_y = first[c]
        to_y.wait_recv()
        part = ef.at[m ^ 4, c]
        out_r, out_l = put(part, part, xr), put(part, part, xl)
        to_r.wait_recv()
        lo = ef.at[m_l, c, pl.ds(0, mid)]
        a = put(lo, lo, xr)
        to_l.wait_recv()
        hi = ef.at[m_r, c, pl.ds(mid, mid)]
        b = put(hi, hi, xl)
        second[c] = (a, b, out_r, out_l)

    def stage3(c):
        second[c][0].wait_recv()
        second[c][1].wait_recv()
        far = ef.at[m_2, c]
        third[c] = put(far, far, y2)

    def rows_in(c):
        second[c][2].wait_recv()
        second[c][3].wait_recv()
        third[c].wait_recv()
        own_pick[c].wait()

    w_sib, w_y, w_own = [None] * 2, [None] * 2, [None] * 2
    wz = [{}, {}]
    from_sib = [[], []]

    def wpair(h, k):
        return wf.at[h, core, (d + k + 8) % 8]

    def w_begin(h):
        mine = wf.at[h, core, d, ylo]
        w_y[h] = put(w_ref.at[h], mine, ypart)
        w_own[h] = keep(w_ref.at[h], mine)

    def w_first(h):
        w_own[h].wait()
        w_y[h].wait_recv()
        both = wpair(h, 0)
        wz[h][1] = put(both, both, zr)
        wz[h][-1] = put(both, both, zl)
        from_sib[h].append(put(both, both, sib))

    def w_step(h, j):
        wz[h][j].wait_recv()
        right = wpair(h, -j)
        if j < 3:
            wz[h][j + 1] = put(right, right, zr)
        else:
            one = right.at[ylo]
            wz[h][4] = put(one, one, zr)
        wz[h][-j].wait_recv()
        left = wpair(h, j)
        if j < 3:
            wz[h][-j - 1] = put(left, left, zl)
        else:
            one = left.at[1 - ylo]
            wz[h][-4] = put(one, one, zl)
        from_sib[h].append(put(right, right, sib))
        from_sib[h].append(put(left, left, sib))

    def w_last(h):
        wz[h][4].wait_recv()
        wz[h][-4].wait_recv()
        far = wpair(h, 4)
        from_sib[h].append(put(far, far, sib))

    def w_in(h):
        for copy in from_sib[h]:
            copy.wait_recv()

    def weight_rows(h, i):
        yy, cc, z0 = i // 4, (i // 2) % 2, (i % 2) * 4
        return [wf[h, cc, z0 + k, yy] for k in range(4)]

    def project(h, c):
        lhs = jnp.concatenate([ef[i, c] for i in range(N_MP)], axis=1)
        rhs = jnp.concatenate([r for i in range(N_MP) for r in weight_rows(h, i)], axis=0)
        out = nn(lhs, rhs).astype(BF16)
        kv[h, c] = out.reshape(DSEQ, CROWS, 2 * HALF)

    def project_range(h, lo, hi):
        def body(c, carry):
            project(h, c)
            return carry

        lax.fori_loop(lo, hi, body, 0)

    def attend_range(h, lo, hi):
        def body(t, carry):
            n, p = t // 2, t % 2
            at_k = pl.ds(pl.multiple_of(p * LANES, LANES), LANES)
            at_v = pl.ds(pl.multiple_of(p * LANES + HALF, LANES), LANES)
            at_q = pl.ds(pl.multiple_of(p * LANES + h * HALF, LANES), LANES)
            k = kv[h, :, n, :, at_k].reshape(SEQ, LANES)
            v = kv[h, :, n, :, at_v].reshape(SEQ, LANES)
            ctx, gq, kt, vt = attend_pair(k, v, q_ref[n, :, at_q], g_ref[n, :, at_q])
            ctx_ref[n, :, at_q] = ctx
            gq_ref[n, :, at_q] = gq
            terms[h, :, n, :, at_k] = kt.reshape(CHUNKS, CROWS, LANES)
            terms[h, :, n, :, at_v] = vt.reshape(CHUNKS, CROWS, LANES)
            return carry

        lax.fori_loop(lo, hi, body, 0)

    def remote(src, dst, ss, rs, to):
        return pltpu.make_async_remote_copy(
            src_ref=src, dst_ref=dst, send_sem=ss, recv_sem=rs, device_id=to, device_id_type=MESH
        )

    def to_sib(h, i):
        return remote(tosib.at[h, i], fromsib.at[h, i], sib_s.at[h, i], sib_r.at[h, i], sib)

    def to_y(h, k):
        return remote(ysend.at[h, k], yrecv.at[h, k], y_s.at[h, k], y_r.at[h, k], ypart)

    def to_p(h, k):
        to = zr if k == 0 else zl
        return remote(psend.at[h, k], precv.at[h, k], p_s.at[h, k], p_r.at[h, k], to)

    half = WROWS // 2

    def to_z(h, k):
        to = zr if k % 2 == 0 else zl
        if k < 2:
            rows = pl.ds(k * half, half)
            return remote(zsend.at[h, k, rows], zrecv.at[h, k, rows], z_s.at[h, k], z_r.at[h, k], to)
        return remote(zsend.at[h, k], zrecv.at[h, k], z_s.at[h, k], z_r.at[h, k], to)

    def columns(yy, cc, dd):
        block = (yy * 2 + cc) * 8 + dd
        at = pl.ds(pl.multiple_of((block % 4) * WROWS, WROWS), WROWS)
        return ef[block // 4, :, :, at].reshape(DSEQ * SEQ, WROWS)

    def block_pair(h, cc, dd):
        e = jnp.concatenate([columns(1 - ylo, cc, dd), columns(ylo, cc, dd)], axis=1)
        return tn(e, terms[h].reshape(DSEQ * SEQ, 2 * HALF))

    def absorb(h, k):
        to_sib(h, k).wait_recv()
        own[h, k] += fromsib[h, k].astype(F32)

    def chain4(h):
        to_y(h, 0).wait_recv()
        total = own[h, 0, WROWS:] + yrecv[h, 0].astype(F32)
        zsend[h, 0, :half] = total[:half].astype(BF16)
        to_z(h, 0).start()
        zsend[h, 1, half:] = total[half:].astype(BF16)
        to_z(h, 1).start()

    def blocks(h):
        def step(i, carry):
            j = (i % 2) * (4 - (i + 1) // 2) + (1 - i % 2) * (4 + i // 2)
            dd = (d + j) % 8
            tosib[h, i] = block_pair(h, 1 - core, dd).astype(BF16)
            to_sib(h, i).start()
            own[h, i] = block_pair(h, core, dd)

            @pl.when(i == 6)
            def _():
                chain4(h)

            @pl.when(i > 0)
            def _():
                absorb(h, i - 1)

            @pl.when((i > 0) & (i < 6))
            def _():
                ysend[h, i - 1] = own[h, i - 1, :WROWS].astype(BF16)
                to_y(h, i - 1).start()

            return carry

        lax.fori_loop(0, 8, step, 0)
        absorb(h, 7)

    def chain3(h):
        to_y(h, 1).wait_recv()
        total = own[h, 1, WROWS:] + yrecv[h, 1].astype(F32)
        to_z(h, 0).wait_recv()
        zsend[h, 2, :half] = (total[:half] + zrecv[h, 0, :half].astype(F32)).astype(BF16)
        zsend[h, 2, half:] = total[half:].astype(BF16)
        to_z(h, 2).start()
        to_y(h, 2).wait_recv()
        total = own[h, 2, WROWS:] + yrecv[h, 2].astype(F32)
        to_z(h, 1).wait_recv()
        zsend[h, 3, :half] = total[:half].astype(BF16)
        zsend[h, 3, half:] = (total[half:] + zrecv[h, 1, half:].astype(F32)).astype(BF16)
        to_z(h, 3).start()
        for k in range(2):
            psend[h, k] = own[h, 5 + k, :WROWS].astype(BF16)
            to_p(h, k).start()

    def chain2(h):
        for k in range(2):
            to_y(h, 3 + k).wait_recv()
            total = own[h, 3 + k, WROWS:] + yrecv[h, 3 + k].astype(F32)
            to_z(h, 2 + k).wait_recv()
            zsend[h, 4 + k] = (total + zrecv[h, 2 + k].astype(F32)).astype(BF16)
            to_z(h, 4 + k).start()

    def partner(h):
        total = own[h, 7, :WROWS]
        for k in range(2):
            to_p(h, k).wait_recv()
            total = total + precv[h, k].astype(F32)
        ysend[h, 5] = total.astype(BF16)
        to_y(h, 5).start()

    def chain1(h):
        for k in range(2):
            to_z(h, 4 + k).wait_recv()
            zsend[h, 6 + k] = (own[h, 5 + k, WROWS:] + zrecv[h, 4 + k].astype(F32)).astype(BF16)
            to_z(h, 6 + k).start()

    def chain0(h):
        total = own[h, 7, WROWS:]
        for k in range(2):
            to_z(h, 6 + k).wait_recv()
            total = total + zrecv[h, 6 + k].astype(F32)
        to_y(h, 5).wait_recv()
        total = total + yrecv[h, 5].astype(F32)
        at = pl.ds(h * HALF, HALF)
        o_ref[0, :, at] = total[:, :HALF]
        o_ref[1, :, at] = total[:, HALF:]

    def drain(h):
        for k in range(8):
            to_sib(h, k).wait_send()
            to_z(h, k).wait_send()
        for k in range(6):
            to_y(h, k).wait_send()
        for k in range(2):
            to_p(h, k).wait_send()

    for c in range(CHUNKS):
        own_slot[c] = keep(snd_ref.at[d, pl.ds(c * CROWS, CROWS)], slots[c].at[d])
    pl.semaphore_wait(barrier, len(peers))
    w_begin(0)
    rows_out(0)
    rows_out(1)
    w_begin(1)
    w_first(0)
    rows_out(2)
    rows_out(3)
    stage1(0)
    stage1(1)
    stage2(0)
    w_step(0, 1)
    stage1(2)
    stage2(1)
    stage3(0)
    stage1(3)
    w_step(0, 2)
    stage2(2)
    stage3(1)
    w_first(1)
    w_step(0, 3)
    stage2(3)
    stage3(2)
    w_step(1, 1)
    w_last(0)
    stage3(3)
    w_in(0)
    for c in range(CHUNKS - 1):
        rows_in(c)
    w_step(1, 2)
    project_range(0, 0, CHUNKS - 1)
    rows_in(CHUNKS - 1)
    project_range(0, CHUNKS - 1, CHUNKS)
    w_step(1, 3)
    attend_range(0, 0, 4)
    w_last(1)
    attend_range(0, 4, 8)
    blocks(0)
    w_in(1)
    project_range(1, 0, 2)
    chain3(0)
    project_range(1, 2, 4)
    chain2(0)
    attend_range(1, 0, 4)
    partner(0)
    chain1(0)
    attend_range(1, 4, 8)
    blocks(1)
    chain0(0)
    chain3(1)
    chain2(1)
    partner(1)
    chain1(1)
    chain0(1)
    for copy in sent:
        copy.wait_send()
    drain(0)
    drain(1)


def run(holder, w_halves, query, grad_context, enc_send):
    rows, inner = WROWS, query.shape[2]
    vmem = pl.BlockSpec(memory_space=pltpu.VMEM)
    dma = pltpu.SemaphoreType.DMA
    wide = 2 * HALF
    return pl.pallas_call(
        kernel,
        out_shape=(
            jax.ShapeDtypeStruct(query.shape, BF16),
            jax.ShapeDtypeStruct(query.shape, BF16),
            jax.ShapeDtypeStruct((2, rows, inner), F32),
        ),
        in_specs=[
            pl.BlockSpec(memory_space=pltpu.SMEM), vmem, vmem, vmem,
            pl.BlockSpec(memory_space=pl.ANY),
        ],
        out_specs=(vmem, vmem, vmem),
        scratch_shapes=[pltpu.VMEM((N_DP, CROWS, SLICE), BF16)] * CHUNKS
        + [pltpu.VMEM((DSEQ * CROWS, SLICE), BF16)] * CHUNKS
        + [
            pltpu.VMEM((N_MP, CHUNKS, DSEQ * CROWS, SLICE), BF16),
            pltpu.VMEM((2, 2, N_DP, 2, rows, wide), BF16),
            pltpu.VMEM((2, CHUNKS, DSEQ, CROWS, wide), BF16),
            pltpu.VMEM((2, CHUNKS, DSEQ, CROWS, wide), BF16),
            pltpu.VMEM((2, 8, 2 * rows, wide), BF16),
            pltpu.VMEM((2, 8, 2 * rows, wide), BF16),
            pltpu.VMEM((2, 8, 2 * rows, wide), F32),
            pltpu.VMEM((2, 6, rows, wide), BF16),
            pltpu.VMEM((2, 6, rows, wide), BF16),
            pltpu.VMEM((2, 2, rows, wide), BF16),
            pltpu.VMEM((2, 2, rows, wide), BF16),
            pltpu.VMEM((2, 8, rows, wide), BF16),
            pltpu.VMEM((2, 8, rows, wide), BF16),
            dma((GATHER_COPIES,)), dma((GATHER_COPIES,)), dma((2 + 2 * CHUNKS,)),
            dma((2, 8)), dma((2, 8)), dma((2, 6)), dma((2, 6)),
            dma((2, 2)), dma((2, 2)), dma((2, 8)), dma((2, 8)),
        ],
        compiler_params=pltpu.CompilerParams(
            collective_id=0, has_side_effects=True, vmem_limit_bytes=60 * 2**20
        ),
        name="cross_attention",
    )(holder, w_halves, query, grad_context, enc_send)


def per_device(encoder_rows, w_key, w_value, query, grad_context, source):
    ex_dev = encoder_rows.shape[0]
    dec_dev, q_rows, inner = query.shape
    s, d, m = lax.axis_index("section"), lax.axis_index("dp"), lax.axis_index("mp")
    per_section = N_DP * dec_dev
    plan = lax.dynamic_slice_in_dim(source, s * per_section, per_section).reshape(N_DP, dec_dev)
    holder_dp = lax.div(plan, jnp.int32(ex_dev)) - s * N_DP
    local_ex = lax.rem(plan, jnp.int32(ex_dev))
    chosen = jnp.sum(jnp.where(holder_dp == d, local_ex, 0), axis=1)
    my_holder = lax.dynamic_index_in_dim(holder_dp, d, 0, keepdims=False)
    columns = lax.dynamic_slice_in_dim(encoder_rows, m * SLICE, SLICE, axis=2)
    enc_send = jnp.take(columns, chosen, axis=0, mode="clip")
    w_halves = jnp.stack(
        [
            jnp.concatenate([w[:, h * HALF : (h + 1) * HALF] for w in (w_key, w_value)], axis=1)
            for h in range(2)
        ]
    )
    return run(my_holder, w_halves, query, grad_context, enc_send)


def solution(mesh):
    return jax.shard_map(
        per_device,
        mesh=mesh,
        in_specs=(
            P(("section", "dp"), None, None),
            P(("section", "dp"), "mp"),
            P(("section", "dp"), "mp"),
            P(("section", "dp"), None, "mp"),
            P(("section", "dp"), None, "mp"),
            P(),
        ),
        out_specs=(
            P(("section", "dp"), None, "mp"),
            P(("section", "dp"), None, "mp"),
            P(None, ("section", "dp"), "mp"),
        ),
        check_vma=False,
    )
```

```python
import jax
import jax.numpy as jnp
from jax import lax
from jax.experimental import pallas as pl
from jax.experimental.pallas import tpu as pltpu
from jax.sharding import PartitionSpec as P

HEAD_DIM = 64
MESH = pl.DeviceIdType.MESH
BF16 = jnp.bfloat16
F32 = jnp.float32
N_DP = 8
N_MP = 8
DSEQ = 4
SEQ = 256
CHUNKS = 8
CROWS = SEQ // CHUNKS
SLICE = 512
WROWS = 128
LANES = 128
EX_DEV = 3
GROUPS = 2
GW = SLICE // GROUPS
PAIRS = GW // LANES
ORDER = (4, 3, 5, 2, 6, 1, 7)
GATHER_COPIES = 15 * CHUNKS + 17 * GROUPS


def nt(a, b):
    return lax.dot_general(a, b, (((1,), (1,)), ((), ())), preferred_element_type=F32)


def nn(a, b):
    return lax.dot_general(a, b, (((1,), (0,)), ((), ())), preferred_element_type=F32)


def tn(a, b):
    return lax.dot_general(a, b, (((0,), (0,)), ((), ())), preferred_element_type=F32)


def attend_pair(k, v, q, g):
    rows = q.shape[0]
    low = lax.broadcasted_iota(jnp.int32, q.shape, 1) < HEAD_DIM
    zero = jnp.zeros_like(q)
    q2 = jnp.concatenate([jnp.where(low, q, zero), jnp.where(low, zero, q)], axis=0)
    g2 = jnp.concatenate([jnp.where(low, g, zero), jnp.where(low, zero, g)], axis=0)
    scores = nt(k, q2)
    expo = jnp.exp(scores - jnp.max(scores, axis=0, keepdims=True))
    weights = expo * (1.0 / jnp.sum(expo, axis=0, keepdims=True))
    probs = weights.astype(BF16)
    dprobs = nt(v, g2)
    delta = jnp.sum(weights * dprobs, axis=0, keepdims=True)
    grads = (weights * (dprobs - delta)).astype(BF16)
    ctx = tn(probs, v)
    gq = tn(grads, k)
    return (
        jnp.where(low, ctx[:rows], ctx[rows:]).astype(BF16),
        jnp.where(low, gq[:rows], gq[rows:]).astype(BF16),
        nn(grads, q2).astype(BF16),
        nn(probs, g2).astype(BF16),
    )


def kernel(src_ref, e_hbm, wk_hbm, wv_hbm, q_hbm, g_hbm, ctx_ref, gq_ref, o_ref, *scratch):
    slots, picks = scratch[0:CHUNKS], scratch[CHUNKS : 2 * CHUNKS]
    (snd, rows_ref, q_ref, g_ref, ef, wf, kv, terms, tosib, fromsib, own, ysend, yrecv, psend,
     precv, zsend, zrecv, ssem, rsem, lsem, sib_s, sib_r, y_s, y_r, p_s, p_r, z_s, z_r) = scratch[
        2 * CHUNKS :
    ]
    s, d, m = lax.axis_index("section"), lax.axis_index("dp"), lax.axis_index("mp")
    core, ylo = s % 2, s // 2
    sib, ypart = (s ^ 1, d, m), (s ^ 2, d, m)
    zr, zl = (s, (d + 1) % 8, m), (s, (d + 7) % 8, m)
    x, yhi = m % 4, m // 4
    m_r, m_l, m_2 = yhi * 4 + (x + 1) % 4, yhi * 4 + (x + 3) % 4, yhi * 4 + (x + 2) % 4
    xr, xl, y2 = (s, d, m_r), (s, d, m_l), (s, d, m ^ 4)

    barrier = pltpu.get_barrier_semaphore()
    peers = [sib, ypart, xr, xl, y2] + [(s, (d + k) % 8, m) for k in range(1, 8)]
    for peer in peers:
        pl.semaphore_signal(barrier, inc=1, device_id=peer, device_id_type=MESH)

    sent, local = [], []

    def put(src, dst, to):
        i = len(sent)
        copy = pltpu.make_async_remote_copy(
            src_ref=src, dst_ref=dst, send_sem=ssem.at[i], recv_sem=rsem.at[i],
            device_id=to, device_id_type=MESH,
        )
        copy.start()
        sent.append(copy)
        return copy

    def keep(src, dst):
        copy = pltpu.make_async_copy(src, dst, lsem.at[len(local)])
        copy.start()
        local.append(copy)
        return copy

    arrive, own_pick = [None] * CHUNKS, [None] * CHUNKS
    first, second, third = [None] * CHUNKS, [None] * CHUNKS, [None] * CHUNKS
    mid = DSEQ * CROWS // 2

    def source_of(reader, n):
        at = src_ref[s * (N_DP * DSEQ) + reader * DSEQ + n]
        return lax.div(at, jnp.int32(EX_DEV)) - s * N_DP, lax.rem(at, jnp.int32(EX_DEV))

    def example_for(reader):
        chosen = jnp.int32(0)
        for n in range(DSEQ):
            holder, example = source_of(reader, n)
            chosen = chosen + jnp.where(holder == d, example, 0)
        return chosen

    def fill():
        for k in range(N_DP):
            chosen = example_for((d + k) % 8)
            for c in range(CHUNKS):
                part = rows_ref[chosen, c * CROWS : (c + 1) * CROWS, :]
                if k:
                    snd[k - 1, c] = part
                else:
                    slots[c][d] = part

    def rows_out(c):
        arrive[c] = [put(snd.at[k - 1, c], slots[c].at[d], (s, (d + k) % 8, m)) for k in ORDER]

    def stage1(c):
        for copy in arrive[c]:
            copy.wait_recv()
        for n in range(DSEQ):
            picks[c][pl.ds(n * CROWS, CROWS), :] = slots[c][holders[n]]
        mine = ef.at[m, c]
        first[c] = (put(picks[c], mine, xr), put(picks[c], mine, xl), put(picks[c], mine, y2))
        own_pick[c] = keep(picks[c], mine)

    def stage2(c):
        to_r, to_l, to_y = first[c]
        to_y.wait_recv()
        part = ef.at[m ^ 4, c]
        out_r, out_l = put(part, part, xr), put(part, part, xl)
        to_r.wait_recv()
        lo = ef.at[m_l, c, pl.ds(0, mid)]
        a = put(lo, lo, xr)
        to_l.wait_recv()
        hi = ef.at[m_r, c, pl.ds(mid, mid)]
        b = put(hi, hi, xl)
        second[c] = (a, b, out_r, out_l)

    def stage3(c):
        second[c][0].wait_recv()
        second[c][1].wait_recv()
        far = ef.at[m_2, c]
        third[c] = put(far, far, y2)

    def rows_in(c):
        second[c][2].wait_recv()
        second[c][3].wait_recv()
        third[c].wait_recv()
        own_pick[c].wait()

    w_y, w_own = [None] * GROUPS, [None] * GROUPS
    wz = [{} for h in range(GROUPS)]
    from_sib = [[] for h in range(GROUPS)]

    def wpair(h, k):
        return wf.at[h, core, (d + k + 8) % 8]

    def w_load(h):
        at = pl.ds(h * GW, GW)
        mine = wf.at[h, core, d, ylo]
        w_own[h] = (
            keep(wk_hbm.at[:, at], mine.at[:, pl.ds(0, GW)]),
            keep(wv_hbm.at[:, at], mine.at[:, pl.ds(GW, GW)]),
        )

    def w_begin(h):
        for copy in w_own[h]:
            copy.wait()
        mine = wf.at[h, core, d, ylo]
        w_y[h] = put(mine, mine, ypart)

    def w_first(h):
        w_y[h].wait_recv()
        both = wpair(h, 0)
        wz[h][1] = put(both, both, zr)
        wz[h][-1] = put(both, both, zl)
        from_sib[h].append(put(both, both, sib))

    def w_step(h, j):
        wz[h][j].wait_recv()
        right = wpair(h, -j)
        if j < 3:
            wz[h][j + 1] = put(right, right, zr)
        else:
            one = right.at[ylo]
            wz[h][4] = put(one, one, zr)
        wz[h][-j].wait_recv()
        left = wpair(h, j)
        if j < 3:
            wz[h][-j - 1] = put(left, left, zl)
        else:
            one = left.at[1 - ylo]
            wz[h][-4] = put(one, one, zl)
        from_sib[h].append(put(right, right, sib))
        from_sib[h].append(put(left, left, sib))

    def w_last(h):
        wz[h][4].wait_recv()
        wz[h][-4].wait_recv()
        far = wpair(h, 4)
        from_sib[h].append(put(far, far, sib))

    def w_in(h):
        for copy in from_sib[h]:
            copy.wait_recv()

    def weight_rows(h, i):
        yy, cc, z0 = i // 4, (i // 2) % 2, (i % 2) * 4
        return [wf[h, cc, z0 + k, yy] for k in range(4)]

    def project(h, c):
        lhs = jnp.concatenate([ef[i, c] for i in range(N_MP)], axis=1)
        rhs = jnp.concatenate([r for i in range(N_MP) for r in weight_rows(h, i)], axis=0)
        out = nn(lhs, rhs).astype(BF16)
        kv[h, c] = out.reshape(DSEQ, CROWS, 2 * GW)

    def project_range(h, lo, hi):
        def body(c, carry):
            project(h, c)
            return carry

        lax.fori_loop(lo, hi, body, 0)

    def attend_range(h, lo, hi):
        def body(t, carry):
            n, p = t // PAIRS, t % PAIRS
            at_k = pl.ds(pl.multiple_of(p * LANES, LANES), LANES)
            at_v = pl.ds(pl.multiple_of(p * LANES + GW, LANES), LANES)
            at_q = pl.ds(pl.multiple_of(p * LANES + h * GW, LANES), LANES)
            k = kv[h, :, n, :, at_k].reshape(SEQ, LANES)
            v = kv[h, :, n, :, at_v].reshape(SEQ, LANES)
            ctx, gq, kt, vt = attend_pair(k, v, q_ref[n, :, at_q], g_ref[n, :, at_q])
            ctx_ref[n, :, at_q] = ctx
            gq_ref[n, :, at_q] = gq
            terms[h, :, n, :, at_k] = kt.reshape(CHUNKS, CROWS, LANES)
            terms[h, :, n, :, at_v] = vt.reshape(CHUNKS, CROWS, LANES)
            return carry

        lax.fori_loop(lo, hi, body, 0)

    def remote(src, dst, ss, rs, to):
        return pltpu.make_async_remote_copy(
            src_ref=src, dst_ref=dst, send_sem=ss, recv_sem=rs, device_id=to, device_id_type=MESH
        )

    def to_sib(h, i):
        return remote(tosib.at[h, i], fromsib.at[h, i], sib_s.at[h, i], sib_r.at[h, i], sib)

    def to_y(h, k):
        return remote(ysend.at[h, k], yrecv.at[h, k], y_s.at[h, k], y_r.at[h, k], ypart)

    def to_p(h, k):
        to = zr if k % 2 == 0 else zl
        return remote(psend.at[h, k], precv.at[h, k], p_s.at[h, k], p_r.at[h, k], to)

    half = WROWS // 2

    def to_z(h, k):
        to = zr if k % 2 == 0 else zl
        if k < 2:
            rows = pl.ds(k * half, half)
            return remote(zsend.at[h, k, rows], zrecv.at[h, k, rows], z_s.at[h, k], z_r.at[h, k], to)
        return remote(zsend.at[h, k], zrecv.at[h, k], z_s.at[h, k], z_r.at[h, k], to)

    def columns(yy, cc, dd):
        block = (yy * 2 + cc) * 8 + dd
        at = pl.ds(pl.multiple_of((block % 4) * WROWS, WROWS), WROWS)
        return ef[block // 4, :, :, at].reshape(DSEQ * SEQ, WROWS)

    def block_pair(h, cc, dd):
        e = jnp.concatenate([columns(1 - ylo, cc, dd), columns(ylo, cc, dd)], axis=1)
        return tn(e, terms[h].reshape(DSEQ * SEQ, 2 * GW))

    def absorb(h, k):
        to_sib(h, k).wait_recv()
        own[h, k] += fromsib[h, k].astype(F32)

    def chain4(h):
        to_y(h, 0).wait_recv()
        total = own[h, 0, WROWS:] + yrecv[h, 0].astype(F32)
        zsend[h, 0, :half] = total[:half].astype(BF16)
        to_z(h, 0).start()
        zsend[h, 1, half:] = total[half:].astype(BF16)
        to_z(h, 1).start()

    def blocks(h):
        def step(i, carry):
            j = (i % 2) * (4 - (i + 1) // 2) + (1 - i % 2) * (4 + i // 2)
            dd = (d + j) % 8
            tosib[h, i] = block_pair(h, 1 - core, dd).astype(BF16)
            to_sib(h, i).start()
            own[h, i] = block_pair(h, core, dd)

            @pl.when(i == 6)
            def _():
                chain4(h)

            @pl.when(i > 0)
            def _():
                absorb(h, i - 1)

            @pl.when((i > 0) & (i < 4))
            def _():
                ysend[h, i - 1] = own[h, i - 1, :WROWS].astype(BF16)
                to_y(h, i - 1).start()

            for k in range(2):

                @pl.when(i == 4 + k)
                def _(k=k):
                    psend[h, k] = own[h, 3 + k, :WROWS].astype(BF16)
                    to_p(h, k).start()

            return carry

        lax.fori_loop(0, 8, step, 0)
        absorb(h, 7)

    def chain3(h):
        to_y(h, 1).wait_recv()
        total = own[h, 1, WROWS:] + yrecv[h, 1].astype(F32)
        to_z(h, 0).wait_recv()
        zsend[h, 2, :half] = (total[:half] + zrecv[h, 0, :half].astype(F32)).astype(BF16)
        zsend[h, 2, half:] = total[half:].astype(BF16)
        to_z(h, 2).start()
        to_y(h, 2).wait_recv()
        total = own[h, 2, WROWS:] + yrecv[h, 2].astype(F32)
        to_z(h, 1).wait_recv()
        zsend[h, 3, :half] = total[:half].astype(BF16)
        zsend[h, 3, half:] = (total[half:] + zrecv[h, 1, half:].astype(F32)).astype(BF16)
        to_z(h, 3).start()
        for k in range(2):
            to_p(h, k).wait_recv()
            psend[h, 2 + k] = (own[h, 5 + k, :WROWS] + precv[h, k].astype(F32)).astype(BF16)
            to_p(h, 2 + k).start()

    def chain2(h):
        for k in range(2):
            to_z(h, 2 + k).wait_recv()
            zsend[h, 4 + k] = (own[h, 3 + k, WROWS:] + zrecv[h, 2 + k].astype(F32)).astype(BF16)
            to_z(h, 4 + k).start()

    def partner(h):
        total = own[h, 7, :WROWS]
        for k in range(2):
            to_p(h, 2 + k).wait_recv()
            total = total + precv[h, 2 + k].astype(F32)
        ysend[h, 3] = total.astype(BF16)
        to_y(h, 3).start()

    def chain1(h):
        for k in range(2):
            to_z(h, 4 + k).wait_recv()
            zsend[h, 6 + k] = (own[h, 5 + k, WROWS:] + zrecv[h, 4 + k].astype(F32)).astype(BF16)
            to_z(h, 6 + k).start()

    def chain0(h):
        total = own[h, 7, WROWS:]
        for k in range(2):
            to_z(h, 6 + k).wait_recv()
            total = total + zrecv[h, 6 + k].astype(F32)
        to_y(h, 3).wait_recv()
        total = total + yrecv[h, 3].astype(F32)
        at = pl.ds(h * GW, GW)
        o_ref[0, :, at] = total[:, :GW]
        o_ref[1, :, at] = total[:, GW:]

    def drain(h):
        for k in range(8):
            to_sib(h, k).wait_send()
            to_z(h, k).wait_send()
        for k in range(4):
            to_y(h, k).wait_send()
            to_p(h, k).wait_send()

    rows_copy = keep(e_hbm.at[:, :, pl.ds(m * SLICE, SLICE)], rows_ref)
    for h in range(GROUPS):
        w_load(h)
    late = (keep(q_hbm, q_ref), keep(g_hbm, g_ref))
    holders = [jnp.clip(source_of(d, n)[0], 0, N_DP - 1) for n in range(DSEQ)]
    rows_copy.wait()
    fill()
    pl.semaphore_wait(barrier, len(peers))
    for h in range(GROUPS):
        w_begin(h)
    for c in range(6):
        rows_out(c)
    w_first(0)
    rows_out(6)
    rows_out(7)
    stage1(0)
    stage2(0)
    stage1(1)
    stage3(0)
    stage2(1)
    stage1(2)
    stage3(1)
    stage1(3)
    stage2(2)
    stage3(2)
    stage1(4)
    stage2(3)
    stage1(5)
    stage3(3)
    stage2(4)
    w_step(0, 1)
    stage3(4)
    stage2(5)
    stage1(6)
    stage3(5)
    stage1(7)
    stage2(6)
    stage3(6)
    w_step(0, 2)
    stage2(7)
    w_first(1)
    stage3(7)
    w_step(0, 3)
    w_step(1, 1)
    w_last(0)
    for c in range(CHUNKS):
        rows_in(c)
    w_in(0)
    project_range(0, 0, CHUNKS)
    w_step(1, 2)
    for copy in late:
        copy.wait()
    attend_range(0, 0, 8)
    w_step(1, 3)
    blocks(0)
    w_last(1)
    w_in(1)
    project_range(1, 0, 4)
    chain3(0)
    project_range(1, 4, 8)
    chain2(0)
    attend_range(1, 0, 4)
    partner(0)
    chain1(0)
    attend_range(1, 4, 8)
    blocks(1)
    chain0(0)
    chain3(1)
    chain2(1)
    partner(1)
    chain1(1)
    chain0(1)
    for copy in sent:
        copy.wait_send()
    for h in range(GROUPS):
        drain(h)


def per_device(encoder_rows, w_key, w_value, query, grad_context, source):
    rows, inner = w_key.shape
    vmem = pl.BlockSpec(memory_space=pltpu.VMEM)
    hbm = pl.BlockSpec(memory_space=pl.ANY)
    dma = pltpu.SemaphoreType.DMA
    wide = 2 * GW
    return pl.pallas_call(
        kernel,
        out_shape=(
            jax.ShapeDtypeStruct(query.shape, BF16),
            jax.ShapeDtypeStruct(query.shape, BF16),
            jax.ShapeDtypeStruct((2, rows, inner), F32),
        ),
        in_specs=[pl.BlockSpec(memory_space=pltpu.SMEM), hbm, hbm, hbm, hbm, hbm],
        out_specs=(vmem, vmem, vmem),
        scratch_shapes=[pltpu.VMEM((N_DP, CROWS, SLICE), BF16)] * CHUNKS
        + [pltpu.VMEM((DSEQ * CROWS, SLICE), BF16)] * CHUNKS
        + [
            pltpu.VMEM((N_DP - 1, CHUNKS, CROWS, SLICE), BF16),
            pltpu.VMEM((EX_DEV, SEQ, SLICE), BF16),
            pltpu.VMEM(query.shape, BF16),
            pltpu.VMEM(query.shape, BF16),
            pltpu.VMEM((N_MP, CHUNKS, DSEQ * CROWS, SLICE), BF16),
            pltpu.VMEM((GROUPS, 2, N_DP, 2, rows, wide), BF16),
            pltpu.VMEM((GROUPS, CHUNKS, DSEQ, CROWS, wide), BF16),
            pltpu.VMEM((GROUPS, CHUNKS, DSEQ, CROWS, wide), BF16),
            pltpu.VMEM((GROUPS, 8, 2 * rows, wide), BF16),
            pltpu.VMEM((GROUPS, 8, 2 * rows, wide), BF16),
            pltpu.VMEM((GROUPS, 8, 2 * rows, wide), F32),
            pltpu.VMEM((GROUPS, 4, rows, wide), BF16),
            pltpu.VMEM((GROUPS, 4, rows, wide), BF16),
            pltpu.VMEM((GROUPS, 4, rows, wide), BF16),
            pltpu.VMEM((GROUPS, 4, rows, wide), BF16),
            pltpu.VMEM((GROUPS, 8, rows, wide), BF16),
            pltpu.VMEM((GROUPS, 8, rows, wide), BF16),
            dma((GATHER_COPIES,)), dma((GATHER_COPIES,)), dma((3 + 2 * GROUPS + CHUNKS,)),
            dma((GROUPS, 8)), dma((GROUPS, 8)), dma((GROUPS, 4)), dma((GROUPS, 4)),
            dma((GROUPS, 4)), dma((GROUPS, 4)), dma((GROUPS, 8)), dma((GROUPS, 8)),
        ],
        compiler_params=pltpu.CompilerParams(
            collective_id=0, has_side_effects=True, vmem_limit_bytes=61 * 2**20
        ),
        name="cross_attention",
    )(source, encoder_rows, w_key, w_value, query, grad_context)


def solution(mesh):
    return jax.shard_map(
        per_device,
        mesh=mesh,
        in_specs=(
            P(("section", "dp"), None, None),
            P(("section", "dp"), "mp"),
            P(("section", "dp"), "mp"),
            P(("section", "dp"), None, "mp"),
            P(("section", "dp"), None, "mp"),
            P(),
        ),
        out_specs=(
            P(("section", "dp"), None, "mp"),
            P(("section", "dp"), None, "mp"),
            P(None, ("section", "dp"), "mp"),
        ),
        check_vma=False,
    )
```

```python
import jax
import jax.numpy as jnp
from jax import lax
from jax.experimental import pallas as pl
from jax.experimental.pallas import tpu as pltpu
from jax.sharding import PartitionSpec as P

HEAD_DIM = 64
MESH = pl.DeviceIdType.MESH
BF16 = jnp.bfloat16
F32 = jnp.float32
N_DP = 8
N_MP = 8
DSEQ = 4
SEQ = 256
CHUNKS = 8
CROWS = SEQ // CHUNKS
SLICE = 512
WROWS = 128
LANES = 128
EX_DEV = 3
GROUPS = 2
GW = SLICE // GROUPS
PAIRS = GW // LANES
ORDER = (4, 3, 5, 2, 6, 1, 7)
LIGHT = (7,)
GATHER_COPIES = 15 * CHUNKS + 2 * len(LIGHT) + 17 * GROUPS


def nt(a, b):
    return lax.dot_general(a, b, (((1,), (1,)), ((), ())), preferred_element_type=F32)


def nn(a, b):
    return lax.dot_general(a, b, (((1,), (0,)), ((), ())), preferred_element_type=F32)


def tn(a, b):
    return lax.dot_general(a, b, (((0,), (0,)), ((), ())), preferred_element_type=F32)


def attend_pair(k, v, q, g):
    rows = q.shape[0]
    low = lax.broadcasted_iota(jnp.int32, q.shape, 1) < HEAD_DIM
    zero = jnp.zeros_like(q)
    q2 = jnp.concatenate([jnp.where(low, q, zero), jnp.where(low, zero, q)], axis=0)
    g2 = jnp.concatenate([jnp.where(low, g, zero), jnp.where(low, zero, g)], axis=0)
    scores = nt(k, q2)
    expo = jnp.exp(scores - jnp.max(scores, axis=0, keepdims=True))
    weights = expo * (1.0 / jnp.sum(expo, axis=0, keepdims=True))
    probs = weights.astype(BF16)
    dprobs = nt(v, g2)
    delta = jnp.sum(weights * dprobs, axis=0, keepdims=True)
    grads = (weights * (dprobs - delta)).astype(BF16)
    ctx = tn(probs, v)
    gq = tn(grads, k)
    return (
        jnp.where(low, ctx[:rows], ctx[rows:]).astype(BF16),
        jnp.where(low, gq[:rows], gq[rows:]).astype(BF16),
        nn(grads, q2).astype(BF16),
        nn(probs, g2).astype(BF16),
    )


def kernel(src_ref, e_hbm, wk_hbm, wv_hbm, q_hbm, g_hbm, ctx_ref, gq_ref, o_ref, *scratch):
    slots, picks = scratch[0:CHUNKS], scratch[CHUNKS : 2 * CHUNKS]
    (snd, rows_ref, q_ref, g_ref, ef, wf, kv, terms, tosib, fromsib, own, ysend, yrecv, psend,
     precv, zsend, zrecv, ssem, rsem, lsem, sib_s, sib_r, y_s, y_r, p_s, p_r, z_s, z_r) = scratch[
        2 * CHUNKS :
    ]
    s, d, m = lax.axis_index("section"), lax.axis_index("dp"), lax.axis_index("mp")
    core, ylo = s % 2, s // 2
    sib, ypart = (s ^ 1, d, m), (s ^ 2, d, m)
    zr, zl = (s, (d + 1) % 8, m), (s, (d + 7) % 8, m)
    x, yhi = m % 4, m // 4
    m_r, m_l, m_2 = yhi * 4 + (x + 1) % 4, yhi * 4 + (x + 3) % 4, yhi * 4 + (x + 2) % 4
    xr, xl, y2 = (s, d, m_r), (s, d, m_l), (s, d, m ^ 4)

    barrier = pltpu.get_barrier_semaphore()
    peers = [sib, ypart, xr, xl, y2] + [(s, (d + k) % 8, m) for k in range(1, 8)]
    for peer in peers:
        pl.semaphore_signal(barrier, inc=1, device_id=peer, device_id_type=MESH)

    sent, local = [], []

    def put(src, dst, to):
        i = len(sent)
        copy = pltpu.make_async_remote_copy(
            src_ref=src, dst_ref=dst, send_sem=ssem.at[i], recv_sem=rsem.at[i],
            device_id=to, device_id_type=MESH,
        )
        copy.start()
        sent.append(copy)
        return copy

    def keep(src, dst):
        copy = pltpu.make_async_copy(src, dst, lsem.at[len(local)])
        copy.start()
        local.append(copy)
        return copy

    arrive, own_pick = [None] * CHUNKS, [None] * CHUNKS
    first, second, third = [None] * CHUNKS, [None] * CHUNKS, [None] * CHUNKS
    mid = DSEQ * CROWS // 2

    def source_of(reader, n):
        at = src_ref[s * (N_DP * DSEQ) + reader * DSEQ + n]
        return lax.div(at, jnp.int32(EX_DEV)) - s * N_DP, lax.rem(at, jnp.int32(EX_DEV))

    def example_for(reader):
        chosen = jnp.int32(0)
        for n in range(DSEQ):
            holder, example = source_of(reader, n)
            chosen = chosen + jnp.where(holder == d, example, 0)
        return chosen

    def fill():
        for k in range(N_DP):
            chosen = example_for((d + k) % 8)
            for c in range(CHUNKS):
                part = rows_ref[chosen, c * CROWS : (c + 1) * CROWS, :]
                if k:
                    snd[k - 1, c] = part
                else:
                    slots[c][d] = part

    def rows_out(c):
        arrive[c] = [put(snd.at[k - 1, c], slots[c].at[d], (s, (d + k) % 8, m)) for k in ORDER]

    def stage1(c):
        for copy in arrive[c]:
            copy.wait_recv()
        for n in range(DSEQ):
            picks[c][pl.ds(n * CROWS, CROWS), :] = slots[c][holders[n]]
        mine = ef.at[m, c]
        first[c] = (put(picks[c], mine, xr), put(picks[c], mine, xl), put(picks[c], mine, y2))
        own_pick[c] = keep(picks[c], mine)

    def stage2(c):
        to_r, to_l, to_y = first[c]
        to_y.wait_recv()
        part = ef.at[m ^ 4, c]
        out_r, out_l = put(part, part, xr), put(part, part, xl)
        to_r.wait_recv()
        lo = ef.at[m_l, c, pl.ds(0, mid)]
        a = put(lo, lo, xr)
        to_l.wait_recv()
        hi = ef.at[m_r, c, pl.ds(mid, mid)]
        b = put(hi, hi, xl)
        second[c] = (a, b, out_r, out_l)

    def stage3(c):
        if c in LIGHT:
            a, b, out_r, out_l = second[c]
            out_r.wait_recv()
            lo = ef.at[m_l ^ 4, c, pl.ds(0, mid)]
            far_a = put(lo, lo, xr)
            out_l.wait_recv()
            hi = ef.at[m_r ^ 4, c, pl.ds(mid, mid)]
            far_b = put(hi, hi, xl)
            third[c] = (a, b, far_a, far_b)
        else:
            second[c][0].wait_recv()
            second[c][1].wait_recv()
            far = ef.at[m_2, c]
            third[c] = (second[c][2], second[c][3], put(far, far, y2))

    def rows_in(c):
        for copy in third[c]:
            copy.wait_recv()
        own_pick[c].wait()

    w_y, w_own = [None] * GROUPS, [None] * GROUPS
    wz = [{} for h in range(GROUPS)]
    from_sib = [[] for h in range(GROUPS)]

    def wpair(h, k):
        return wf.at[h, core, (d + k + 8) % 8]

    def w_load(h):
        at = pl.ds(h * GW, GW)
        mine = wf.at[h, core, d, ylo]
        w_own[h] = (
            keep(wk_hbm.at[:, at], mine.at[:, pl.ds(0, GW)]),
            keep(wv_hbm.at[:, at], mine.at[:, pl.ds(GW, GW)]),
        )

    def w_begin(h):
        for copy in w_own[h]:
            copy.wait()
        mine = wf.at[h, core, d, ylo]
        w_y[h] = put(mine, mine, ypart)

    def w_first(h):
        w_y[h].wait_recv()
        both = wpair(h, 0)
        wz[h][1] = put(both, both, zr)
        wz[h][-1] = put(both, both, zl)
        from_sib[h].append(put(both, both, sib))

    def w_step(h, j):
        wz[h][j].wait_recv()
        right = wpair(h, -j)
        if j < 3:
            wz[h][j + 1] = put(right, right, zr)
        else:
            one = right.at[ylo]
            wz[h][4] = put(one, one, zr)
        wz[h][-j].wait_recv()
        left = wpair(h, j)
        if j < 3:
            wz[h][-j - 1] = put(left, left, zl)
        else:
            one = left.at[1 - ylo]
            wz[h][-4] = put(one, one, zl)
        from_sib[h].append(put(right, right, sib))
        from_sib[h].append(put(left, left, sib))

    def w_last(h):
        wz[h][4].wait_recv()
        wz[h][-4].wait_recv()
        far = wpair(h, 4)
        from_sib[h].append(put(far, far, sib))

    def w_in(h):
        for copy in from_sib[h]:
            copy.wait_recv()

    def weight_rows(h, i):
        yy, cc, z0 = i // 4, (i // 2) % 2, (i % 2) * 4
        return [wf[h, cc, z0 + k, yy] for k in range(4)]

    def project_range(h, lo, hi):
        rows = (hi - lo) * DSEQ * CROWS
        lhs = jnp.concatenate([ef[i, lo:hi].reshape(rows, SLICE) for i in range(N_MP)], axis=1)
        rhs = jnp.concatenate([r for i in range(N_MP) for r in weight_rows(h, i)], axis=0)
        kv[h, lo:hi] = nn(lhs, rhs).astype(BF16).reshape(hi - lo, DSEQ, CROWS, 2 * GW)

    def attend_range(h, lo, hi):
        def body(t, carry):
            n, p = t // PAIRS, t % PAIRS
            at_k = pl.ds(pl.multiple_of(p * LANES, LANES), LANES)
            at_v = pl.ds(pl.multiple_of(p * LANES + GW, LANES), LANES)
            at_q = pl.ds(pl.multiple_of(p * LANES + h * GW, LANES), LANES)
            k = kv[h, :, n, :, at_k].reshape(SEQ, LANES)
            v = kv[h, :, n, :, at_v].reshape(SEQ, LANES)
            ctx, gq, kt, vt = attend_pair(k, v, q_ref[n, :, at_q], g_ref[n, :, at_q])
            ctx_ref[n, :, at_q] = ctx
            gq_ref[n, :, at_q] = gq
            terms[h, :, n, :, at_k] = kt.reshape(CHUNKS, CROWS, LANES)
            terms[h, :, n, :, at_v] = vt.reshape(CHUNKS, CROWS, LANES)
            return carry

        lax.fori_loop(lo, hi, body, 0)

    def remote(src, dst, ss, rs, to):
        return pltpu.make_async_remote_copy(
            src_ref=src, dst_ref=dst, send_sem=ss, recv_sem=rs, device_id=to, device_id_type=MESH
        )

    def to_sib(h, i):
        return remote(tosib.at[h, i], fromsib.at[h, i], sib_s.at[h, i], sib_r.at[h, i], sib)

    def to_y(h, k):
        return remote(ysend.at[h, k], yrecv.at[h, k], y_s.at[h, k], y_r.at[h, k], ypart)

    def to_p(h, k):
        to = zr if k % 2 == 0 else zl
        return remote(psend.at[h, k], precv.at[h, k], p_s.at[h, k], p_r.at[h, k], to)

    half = WROWS // 2

    def to_z(h, k):
        to = zr if k % 2 == 0 else zl
        if k < 2:
            rows = pl.ds(k * half, half)
            return remote(zsend.at[h, k, rows], zrecv.at[h, k, rows], z_s.at[h, k], z_r.at[h, k], to)
        return remote(zsend.at[h, k], zrecv.at[h, k], z_s.at[h, k], z_r.at[h, k], to)

    def columns(yy, cc, dd):
        block = (yy * 2 + cc) * 8 + dd
        at = pl.ds(pl.multiple_of((block % 4) * WROWS, WROWS), WROWS)
        return ef[block // 4, :, :, at].reshape(DSEQ * SEQ, WROWS)

    def block_pair(h, cc, dd):
        e = jnp.concatenate([columns(1 - ylo, cc, dd), columns(ylo, cc, dd)], axis=1)
        return tn(e, terms[h].reshape(DSEQ * SEQ, 2 * GW))

    def absorb(h, k):
        to_sib(h, k).wait_recv()
        own[h, k] += fromsib[h, k].astype(F32)

    def chain4(h):
        to_y(h, 0).wait_recv()
        total = own[h, 0, WROWS:] + yrecv[h, 0].astype(F32)
        zsend[h, 0, :half] = total[:half].astype(BF16)
        to_z(h, 0).start()
        zsend[h, 1, half:] = total[half:].astype(BF16)
        to_z(h, 1).start()

    def blocks(h):
        def step(i, carry):
            j = (i % 2) * (4 - (i + 1) // 2) + (1 - i % 2) * (4 + i // 2)
            dd = (d + j) % 8
            tosib[h, i] = block_pair(h, 1 - core, dd).astype(BF16)
            to_sib(h, i).start()
            own[h, i] = block_pair(h, core, dd)

            @pl.when(i == 6)
            def _():
                chain4(h)

            @pl.when(i > 0)
            def _():
                absorb(h, i - 1)

            @pl.when((i > 0) & (i < 4))
            def _():
                ysend[h, i - 1] = own[h, i - 1, :WROWS].astype(BF16)
                to_y(h, i - 1).start()

            for k in range(2):

                @pl.when(i == 4 + k)
                def _(k=k):
                    psend[h, k] = own[h, 3 + k, :WROWS].astype(BF16)
                    to_p(h, k).start()

            return carry

        lax.fori_loop(0, 8, step, 0)
        absorb(h, 7)

    def chain3(h):
        to_y(h, 1).wait_recv()
        total = own[h, 1, WROWS:] + yrecv[h, 1].astype(F32)
        to_z(h, 0).wait_recv()
        zsend[h, 2, :half] = (total[:half] + zrecv[h, 0, :half].astype(F32)).astype(BF16)
        zsend[h, 2, half:] = total[half:].astype(BF16)
        to_z(h, 2).start()
        to_y(h, 2).wait_recv()
        total = own[h, 2, WROWS:] + yrecv[h, 2].astype(F32)
        to_z(h, 1).wait_recv()
        zsend[h, 3, :half] = total[:half].astype(BF16)
        zsend[h, 3, half:] = (total[half:] + zrecv[h, 1, half:].astype(F32)).astype(BF16)
        to_z(h, 3).start()
        for k in range(2):
            to_p(h, k).wait_recv()
            psend[h, 2 + k] = (own[h, 5 + k, :WROWS] + precv[h, k].astype(F32)).astype(BF16)
            to_p(h, 2 + k).start()

    def chain2(h):
        for k in range(2):
            to_z(h, 2 + k).wait_recv()
            zsend[h, 4 + k] = (own[h, 3 + k, WROWS:] + zrecv[h, 2 + k].astype(F32)).astype(BF16)
            to_z(h, 4 + k).start()

    def partner(h):
        total = own[h, 7, :WROWS]
        for k in range(2):
            to_p(h, 2 + k).wait_recv()
            total = total + precv[h, 2 + k].astype(F32)
        ysend[h, 3] = total.astype(BF16)
        to_y(h, 3).start()

    def chain1(h):
        for k in range(2):
            to_z(h, 4 + k).wait_recv()
            zsend[h, 6 + k] = (own[h, 5 + k, WROWS:] + zrecv[h, 4 + k].astype(F32)).astype(BF16)
            to_z(h, 6 + k).start()

    def chain0(h):
        total = own[h, 7, WROWS:]
        for k in range(2):
            to_z(h, 6 + k).wait_recv()
            total = total + zrecv[h, 6 + k].astype(F32)
        to_y(h, 3).wait_recv()
        total = total + yrecv[h, 3].astype(F32)
        at = pl.ds(h * GW, GW)
        o_ref[0, :, at] = total[:, :GW]
        o_ref[1, :, at] = total[:, GW:]

    def drain(h):
        for k in range(8):
            to_sib(h, k).wait_send()
            to_z(h, k).wait_send()
        for k in range(4):
            to_y(h, k).wait_send()
            to_p(h, k).wait_send()

    rows_copy = keep(e_hbm.at[:, :, pl.ds(m * SLICE, SLICE)], rows_ref)
    for h in range(GROUPS):
        w_load(h)
    late = (keep(q_hbm, q_ref), keep(g_hbm, g_ref))
    holders = [jnp.clip(source_of(d, n)[0], 0, N_DP - 1) for n in range(DSEQ)]
    rows_copy.wait()
    fill()
    pl.semaphore_wait(barrier, len(peers))
    rows_out(0)
    rows_out(1)
    rows_out(2)
    rows_out(3)
    rows_out(4)
    rows_out(5)
    w_begin(0)
    w_begin(1)
    w_first(0)
    rows_out(6)
    rows_out(7)
    stage1(0)
    stage1(1)
    stage2(0)
    stage1(2)
    stage2(1)
    stage3(0)
    stage1(3)
    stage2(2)
    rows_in(0)
    stage3(1)
    stage1(4)
    stage2(3)
    rows_in(1)
    stage1(5)
    stage3(2)
    stage2(4)
    w_step(0, 1)
    w_first(1)
    stage3(3)
    rows_in(2)
    stage2(5)
    stage1(6)
    rows_in(3)
    stage3(4)
    stage1(7)
    stage3(5)
    rows_in(4)
    w_step(0, 2)
    stage2(6)
    stage2(7)
    rows_in(5)
    w_step(1, 1)
    stage3(6)
    stage3(7)
    w_step(0, 3)
    rows_in(6)
    rows_in(7)
    w_step(1, 2)
    w_last(0)
    w_in(0)
    project_range(0, 0, 4)
    project_range(0, 4, 7)
    project_range(0, 7, 8)
    for copy in late:
        copy.wait()
    attend_range(0, 0, 2)
    w_step(1, 3)
    attend_range(0, 2, 4)
    attend_range(0, 4, 6)
    attend_range(0, 6, 8)
    blocks(0)
    w_last(1)
    w_in(1)
    project_range(1, 0, 4)
    project_range(1, 4, 8)
    attend_range(1, 0, 2)
    chain3(0)
    attend_range(1, 2, 4)
    attend_range(1, 4, 6)
    attend_range(1, 6, 8)
    blocks(1)
    chain2(0)
    partner(0)
    chain3(1)
    chain1(0)
    chain2(1)
    partner(1)
    chain0(0)
    chain1(1)
    chain0(1)
    for copy in sent:
        copy.wait_send()
    for h in range(GROUPS):
        drain(h)


def hand_over(*refs):
    for i in range(3):
        refs[3 + i][...] = refs[i][...]


def per_device(encoder_rows, w_key, w_value, query, grad_context, source):
    rows, inner = w_key.shape
    vmem = pl.BlockSpec(memory_space=pltpu.VMEM)
    hbm = pl.BlockSpec(memory_space=pl.ANY)
    dma = pltpu.SemaphoreType.DMA
    wide = 2 * GW
    outs = pl.pallas_call(
        kernel,
        out_shape=(
            jax.ShapeDtypeStruct(query.shape, BF16),
            jax.ShapeDtypeStruct(query.shape, BF16),
            jax.ShapeDtypeStruct((2, rows, inner), F32),
        ),
        in_specs=[pl.BlockSpec(memory_space=pltpu.SMEM), hbm, hbm, hbm, hbm, hbm],
        out_specs=(vmem, vmem, vmem),
        scratch_shapes=[pltpu.VMEM((N_DP, CROWS, SLICE), BF16)] * CHUNKS
        + [pltpu.VMEM((DSEQ * CROWS, SLICE), BF16)] * CHUNKS
        + [
            pltpu.VMEM((N_DP - 1, CHUNKS, CROWS, SLICE), BF16),
            pltpu.VMEM((EX_DEV, SEQ, SLICE), BF16),
            pltpu.VMEM(query.shape, BF16),
            pltpu.VMEM(query.shape, BF16),
            pltpu.VMEM((N_MP, CHUNKS, DSEQ * CROWS, SLICE), BF16),
            pltpu.VMEM((GROUPS, 2, N_DP, 2, rows, wide), BF16),
            pltpu.VMEM((GROUPS, CHUNKS, DSEQ, CROWS, wide), BF16),
            pltpu.VMEM((GROUPS, CHUNKS, DSEQ, CROWS, wide), BF16),
            pltpu.VMEM((GROUPS, 8, 2 * rows, wide), BF16),
            pltpu.VMEM((GROUPS, 8, 2 * rows, wide), BF16),
            pltpu.VMEM((GROUPS, 8, 2 * rows, wide), F32),
            pltpu.VMEM((GROUPS, 4, rows, wide), BF16),
            pltpu.VMEM((GROUPS, 4, rows, wide), BF16),
            pltpu.VMEM((GROUPS, 4, rows, wide), BF16),
            pltpu.VMEM((GROUPS, 4, rows, wide), BF16),
            pltpu.VMEM((GROUPS, 8, rows, wide), BF16),
            pltpu.VMEM((GROUPS, 8, rows, wide), BF16),
            dma((GATHER_COPIES,)), dma((GATHER_COPIES,)), dma((3 + 2 * GROUPS + CHUNKS,)),
            dma((GROUPS, 8)), dma((GROUPS, 8)), dma((GROUPS, 4)), dma((GROUPS, 4)),
            dma((GROUPS, 4)), dma((GROUPS, 4)), dma((GROUPS, 8)), dma((GROUPS, 8)),
        ],
        compiler_params=pltpu.CompilerParams(
            collective_id=0, has_side_effects=True, vmem_limit_bytes=61 * 2**20
        ),
        name="cross_attention",
    )(source, encoder_rows, w_key, w_value, query, grad_context)
    return pl.pallas_call(
        hand_over,
        out_shape=tuple(jax.ShapeDtypeStruct(o.shape, o.dtype) for o in outs),
        in_specs=[vmem] * 3,
        out_specs=(vmem,) * 3,
        name="hand_over",
    )(*outs)


def solution(mesh):
    return jax.shard_map(
        per_device,
        mesh=mesh,
        in_specs=(
            P(("section", "dp"), None, None),
            P(("section", "dp"), "mp"),
            P(("section", "dp"), "mp"),
            P(("section", "dp"), None, "mp"),
            P(("section", "dp"), None, "mp"),
            P(),
        ),
        out_specs=(
            P(("section", "dp"), None, "mp"),
            P(("section", "dp"), None, "mp"),
            P(None, ("section", "dp"), "mp"),
        ),
        check_vma=False,
    )
```

```python
import jax
import jax.numpy as jnp
from jax import lax
from jax.experimental import pallas as pl
from jax.experimental.pallas import tpu as pltpu
from jax.sharding import PartitionSpec as P

HEAD_DIM = 64
MESH = pl.DeviceIdType.MESH
BF16 = jnp.bfloat16
F32 = jnp.float32
N_DP = 8
N_MP = 8
DSEQ = 4
SEQ = 256
CHUNKS = 8
CROWS = SEQ // CHUNKS
SLICE = 512
WROWS = 128
LANES = 128
EX_DEV = 3
GROUPS = 2
GW = SLICE // GROUPS
PAIRS = GW // LANES
ON_Z = (2, 3,)
ORDER = (4, 3, 5, 2, 6, 1, 7)
LIGHT = (7,)
GATHER_COPIES = 15 * CHUNKS + 2 * len(LIGHT) + 27 * GROUPS


def nt(a, b):
    return lax.dot_general(a, b, (((1,), (1,)), ((), ())), preferred_element_type=F32)


def nn(a, b):
    return lax.dot_general(a, b, (((1,), (0,)), ((), ())), preferred_element_type=F32)


def tn(a, b):
    return lax.dot_general(a, b, (((0,), (0,)), ((), ())), preferred_element_type=F32)


def attend_pair(k, v, q, g):
    rows = q.shape[0]
    low = lax.broadcasted_iota(jnp.int32, q.shape, 1) < HEAD_DIM
    zero = jnp.zeros_like(q)
    q2 = jnp.concatenate([jnp.where(low, q, zero), jnp.where(low, zero, q)], axis=0)
    g2 = jnp.concatenate([jnp.where(low, g, zero), jnp.where(low, zero, g)], axis=0)
    scores = nt(k, q2)
    expo = jnp.exp(scores - jnp.max(scores, axis=0, keepdims=True))
    weights = expo * (1.0 / jnp.sum(expo, axis=0, keepdims=True))
    probs = weights.astype(BF16)
    dprobs = nt(v, g2)
    delta = jnp.sum(weights * dprobs, axis=0, keepdims=True)
    grads = (weights * (dprobs - delta)).astype(BF16)
    ctx = tn(probs, v)
    gq = tn(grads, k)
    return (
        jnp.where(low, ctx[:rows], ctx[rows:]).astype(BF16),
        jnp.where(low, gq[:rows], gq[rows:]).astype(BF16),
        nn(grads, q2).astype(BF16),
        nn(probs, g2).astype(BF16),
    )


def kernel(src_ref, e_hbm, wk_hbm, wv_hbm, q_hbm, g_hbm, ctx_ref, gq_ref, o_ref, *scratch):
    slots, picks = scratch[0:CHUNKS], scratch[CHUNKS : 2 * CHUNKS]
    (snd, rows_ref, q_ref, g_ref, ef, wf, kv, terms, tosib, fromsib, own, ysend, yrecv, psend,
     precv, zsend, zrecv, ssem, rsem, lsem, sib_s, sib_r, y_s, y_r, p_s, p_r, z_s, z_r) = scratch[
        2 * CHUNKS :
    ]
    s, d, m = lax.axis_index("section"), lax.axis_index("dp"), lax.axis_index("mp")
    core, ylo = s % 2, s // 2
    sib, ypart = (s ^ 1, d, m), (s ^ 2, d, m)
    zr, zl = (s, (d + 1) % 8, m), (s, (d + 7) % 8, m)
    x, yhi = m % 4, m // 4
    m_r, m_l, m_2 = yhi * 4 + (x + 1) % 4, yhi * 4 + (x + 3) % 4, yhi * 4 + (x + 2) % 4
    xr, xl, y2 = (s, d, m_r), (s, d, m_l), (s, d, m ^ 4)

    barrier = pltpu.get_barrier_semaphore()
    peers = [sib, ypart, xr, xl, y2] + [(s, (d + k) % 8, m) for k in range(1, 8)]
    for peer in peers:
        pl.semaphore_signal(barrier, inc=1, device_id=peer, device_id_type=MESH)

    sent, local = [], []

    def put(src, dst, to):
        i = len(sent)
        copy = pltpu.make_async_remote_copy(
            src_ref=src, dst_ref=dst, send_sem=ssem.at[i], recv_sem=rsem.at[i],
            device_id=to, device_id_type=MESH,
        )
        copy.start()
        sent.append(copy)
        return copy

    def keep(src, dst):
        copy = pltpu.make_async_copy(src, dst, lsem.at[len(local)])
        copy.start()
        local.append(copy)
        return copy

    arrive, own_pick = [None] * CHUNKS, [None] * CHUNKS
    first, second, third = [None] * CHUNKS, [None] * CHUNKS, [None] * CHUNKS
    mid = DSEQ * CROWS // 2

    def source_of(reader, n):
        at = src_ref[s * (N_DP * DSEQ) + reader * DSEQ + n]
        return lax.div(at, jnp.int32(EX_DEV)) - s * N_DP, lax.rem(at, jnp.int32(EX_DEV))

    def example_for(reader):
        chosen = jnp.int32(0)
        for n in range(DSEQ):
            holder, example = source_of(reader, n)
            chosen = chosen + jnp.where(holder == d, example, 0)
        return chosen

    def fill():
        for k in range(N_DP):
            chosen = example_for((d + k) % 8)
            for c in range(CHUNKS):
                part = rows_ref[chosen, c * CROWS : (c + 1) * CROWS, :]
                if k:
                    snd[k - 1, c] = part
                else:
                    slots[c][d] = part

    def rows_out(c):
        arrive[c] = [put(snd.at[k - 1, c], slots[c].at[d], (s, (d + k) % 8, m)) for k in ORDER]

    def stage1(c):
        for copy in arrive[c]:
            copy.wait_recv()
        for n in range(DSEQ):
            picks[c][pl.ds(n * CROWS, CROWS), :] = slots[c][holders[n]]
        mine = ef.at[m, c]
        first[c] = (put(picks[c], mine, xr), put(picks[c], mine, xl), put(picks[c], mine, y2))
        own_pick[c] = keep(picks[c], mine)

    def stage2(c):
        to_r, to_l, to_y = first[c]
        to_y.wait_recv()
        part = ef.at[m ^ 4, c]
        out_r, out_l = put(part, part, xr), put(part, part, xl)
        to_r.wait_recv()
        lo = ef.at[m_l, c, pl.ds(0, mid)]
        a = put(lo, lo, xr)
        to_l.wait_recv()
        hi = ef.at[m_r, c, pl.ds(mid, mid)]
        b = put(hi, hi, xl)
        second[c] = (a, b, out_r, out_l)

    def stage3(c):
        if c in LIGHT:
            a, b, out_r, out_l = second[c]
            out_r.wait_recv()
            lo = ef.at[m_l ^ 4, c, pl.ds(0, mid)]
            far_a = put(lo, lo, xr)
            out_l.wait_recv()
            hi = ef.at[m_r ^ 4, c, pl.ds(mid, mid)]
            far_b = put(hi, hi, xl)
            third[c] = (a, b, far_a, far_b)
        else:
            second[c][0].wait_recv()
            second[c][1].wait_recv()
            far = ef.at[m_2, c]
            third[c] = (second[c][2], second[c][3], put(far, far, y2))

    def rows_in(c):
        for copy in third[c]:
            copy.wait_recv()
        own_pick[c].wait()

    w_y, w_own = [None] * GROUPS, [None] * GROUPS
    wz = [{} for h in range(GROUPS)]
    from_sib = [[] for h in range(GROUPS)]
    w_yrecv = [{} for h in range(GROUPS)]

    def wpair(h, k):
        return wf.at[h, core, (d + k + 8) % 8]

    def w_load(h):
        at = pl.ds(h * GW, GW)
        mine = wf.at[h, core, d, ylo]
        w_own[h] = (
            keep(wk_hbm.at[:, at], mine.at[:, pl.ds(0, GW)]),
            keep(wv_hbm.at[:, at], mine.at[:, pl.ds(GW, GW)]),
        )

    def w_begin(h):
        for copy in w_own[h]:
            copy.wait()
        mine = wf.at[h, core, d, ylo]
        w_y[h] = put(mine, mine, ypart)

    def w_first(h):
        w_y[h].wait_recv()
        both = wpair(h, 0)
        wz[h][1] = put(both, both, zr)
        wz[h][-1] = put(both, both, zl)
        from_sib[h].append(put(both, both, sib))

    def w_next(h, j, blk, row, rows, to):
        if j + 1 <= ON_Z[h]:
            return put(blk, blk, to)
        one = blk.at[row] if j < 3 or ON_Z[h] == 3 else blk.at[ylo, rows]
        return put(one, one, to)

    def w_step(h, j):
        half_rows = WROWS // 2
        wz[h][j].wait_recv()
        right = wpair(h, -j)
        wz[h][j + 1] = w_next(h, j, right, ylo, pl.ds(0, half_rows), zr)
        wz[h][-j].wait_recv()
        left = wpair(h, j)
        row = 1 - ylo if j == 3 and ON_Z[h] == 3 else ylo
        wz[h][-j - 1] = w_next(h, j, left, row, pl.ds(half_rows, half_rows), zl)
        for k, blk in ((j, right), (-j, left)):
            if j > ON_Z[h]:
                one = blk.at[ylo]
                w_yrecv[h][k] = put(one, one, ypart)
                blk = one
            from_sib[h].append(put(blk, blk, sib))

    def w_last(h):
        wz[h][4].wait_recv()
        wz[h][-4].wait_recv()
        far = wpair(h, 4)
        if ON_Z[h] < 3:
            far = far.at[ylo]
            w_yrecv[h][4] = put(far, far, ypart)
        from_sib[h].append(put(far, far, sib))

    def w_side(h, k):
        w_yrecv[h][k].wait_recv()
        blk = wpair(h, -k).at[1 - ylo]
        from_sib[h].append(put(blk, blk, sib))

    def w_in(h):
        for copy in from_sib[h]:
            copy.wait_recv()

    def weight_rows(h, i):
        yy, cc, z0 = i // 4, (i // 2) % 2, (i % 2) * 4
        return [wf[h, cc, z0 + k, yy] for k in range(4)]

    def project_range(h, lo, hi):
        rows = (hi - lo) * DSEQ * CROWS
        lhs = jnp.concatenate([ef[i, lo:hi].reshape(rows, SLICE) for i in range(N_MP)], axis=1)
        rhs = jnp.concatenate([r for i in range(N_MP) for r in weight_rows(h, i)], axis=0)
        kv[h, lo:hi] = nn(lhs, rhs).astype(BF16).reshape(hi - lo, DSEQ, CROWS, 2 * GW)

    def attend_range(h, lo, hi):
        def body(t, carry):
            n, p = t // PAIRS, t % PAIRS
            at_k = pl.ds(pl.multiple_of(p * LANES, LANES), LANES)
            at_v = pl.ds(pl.multiple_of(p * LANES + GW, LANES), LANES)
            at_q = pl.ds(pl.multiple_of(p * LANES + h * GW, LANES), LANES)
            k = kv[h, :, n, :, at_k].reshape(SEQ, LANES)
            v = kv[h, :, n, :, at_v].reshape(SEQ, LANES)
            ctx, gq, kt, vt = attend_pair(k, v, q_ref[n, :, at_q], g_ref[n, :, at_q])
            ctx_ref[n, :, at_q] = ctx
            gq_ref[n, :, at_q] = gq
            terms[h, :, n, :, at_k] = kt.reshape(CHUNKS, CROWS, LANES)
            terms[h, :, n, :, at_v] = vt.reshape(CHUNKS, CROWS, LANES)
            return carry

        lax.fori_loop(lo, hi, body, 0)

    def remote(src, dst, ss, rs, to):
        return pltpu.make_async_remote_copy(
            src_ref=src, dst_ref=dst, send_sem=ss, recv_sem=rs, device_id=to, device_id_type=MESH
        )

    def to_sib(h, i):
        return remote(tosib.at[h, i], fromsib.at[h, i], sib_s.at[h, i], sib_r.at[h, i], sib)

    def to_y(h, k):
        return remote(ysend.at[h, k], yrecv.at[h, k], y_s.at[h, k], y_r.at[h, k], ypart)

    def to_p(h, k):
        to = zr if k % 2 == 0 else zl
        return remote(psend.at[h, k], precv.at[h, k], p_s.at[h, k], p_r.at[h, k], to)

    half = WROWS // 2

    def to_z(h, k):
        to = zr if k % 2 == 0 else zl
        if k < 2:
            rows = pl.ds(k * half, half)
            return remote(zsend.at[h, k, rows], zrecv.at[h, k, rows], z_s.at[h, k], z_r.at[h, k], to)
        return remote(zsend.at[h, k], zrecv.at[h, k], z_s.at[h, k], z_r.at[h, k], to)

    def columns(yy, cc, dd):
        block = (yy * 2 + cc) * 8 + dd
        at = pl.ds(pl.multiple_of((block % 4) * WROWS, WROWS), WROWS)
        return ef[block // 4, :, :, at].reshape(DSEQ * SEQ, WROWS)

    def block_pair(h, cc, dd):
        e = jnp.concatenate([columns(1 - ylo, cc, dd), columns(ylo, cc, dd)], axis=1)
        return tn(e, terms[h].reshape(DSEQ * SEQ, 2 * GW))

    def absorb(h, k):
        to_sib(h, k).wait_recv()
        own[h, k] += fromsib[h, k].astype(F32)

    def chain4(h):
        to_y(h, 0).wait_recv()
        total = own[h, 0, WROWS:] + yrecv[h, 0].astype(F32)
        zsend[h, 0, :half] = total[:half].astype(BF16)
        to_z(h, 0).start()
        zsend[h, 1, half:] = total[half:].astype(BF16)
        to_z(h, 1).start()

    def blocks(h):
        def step(i, carry):
            j = (i % 2) * (4 - (i + 1) // 2) + (1 - i % 2) * (4 + i // 2)
            dd = (d + j) % 8
            tosib[h, i] = block_pair(h, 1 - core, dd).astype(BF16)
            to_sib(h, i).start()
            own[h, i] = block_pair(h, core, dd)

            @pl.when(i == 6)
            def _():
                chain4(h)

            @pl.when(i > 0)
            def _():
                absorb(h, i - 1)

            @pl.when((i > 0) & (i < 4))
            def _():
                ysend[h, i - 1] = own[h, i - 1, :WROWS].astype(BF16)
                to_y(h, i - 1).start()

            for k in range(2):

                @pl.when(i == 4 + k)
                def _(k=k):
                    psend[h, k] = own[h, 3 + k, :WROWS].astype(BF16)
                    to_p(h, k).start()

            return carry

        lax.fori_loop(0, 8, step, 0)
        absorb(h, 7)

    def chain3(h):
        to_y(h, 1).wait_recv()
        total = own[h, 1, WROWS:] + yrecv[h, 1].astype(F32)
        to_z(h, 0).wait_recv()
        zsend[h, 2, :half] = (total[:half] + zrecv[h, 0, :half].astype(F32)).astype(BF16)
        zsend[h, 2, half:] = total[half:].astype(BF16)
        to_z(h, 2).start()
        to_y(h, 2).wait_recv()
        total = own[h, 2, WROWS:] + yrecv[h, 2].astype(F32)
        to_z(h, 1).wait_recv()
        zsend[h, 3, :half] = total[:half].astype(BF16)
        zsend[h, 3, half:] = (total[half:] + zrecv[h, 1, half:].astype(F32)).astype(BF16)
        to_z(h, 3).start()
        for k in range(2):
            to_p(h, k).wait_recv()
            psend[h, 2 + k] = (own[h, 5 + k, :WROWS] + precv[h, k].astype(F32)).astype(BF16)
            to_p(h, 2 + k).start()

    def chain2(h):
        for k in range(2):
            to_z(h, 2 + k).wait_recv()
            zsend[h, 4 + k] = (own[h, 3 + k, WROWS:] + zrecv[h, 2 + k].astype(F32)).astype(BF16)
            to_z(h, 4 + k).start()

    def partner(h):
        total = own[h, 7, :WROWS]
        for k in range(2):
            to_p(h, 2 + k).wait_recv()
            total = total + precv[h, 2 + k].astype(F32)
        ysend[h, 3] = total.astype(BF16)
        to_y(h, 3).start()

    def chain1(h):
        for k in range(2):
            to_z(h, 4 + k).wait_recv()
            zsend[h, 6 + k] = (own[h, 5 + k, WROWS:] + zrecv[h, 4 + k].astype(F32)).astype(BF16)
            to_z(h, 6 + k).start()

    def chain0(h):
        total = own[h, 7, WROWS:]
        for k in range(2):
            to_z(h, 6 + k).wait_recv()
            total = total + zrecv[h, 6 + k].astype(F32)
        to_y(h, 3).wait_recv()
        total = total + yrecv[h, 3].astype(F32)
        at = pl.ds(h * GW, GW)
        o_ref[0, :, at] = total[:, :GW]
        o_ref[1, :, at] = total[:, GW:]

    def drain(h):
        for k in range(8):
            to_sib(h, k).wait_send()
            to_z(h, k).wait_send()
        for k in range(4):
            to_y(h, k).wait_send()
            to_p(h, k).wait_send()

    rows_copy = keep(e_hbm.at[:, :, pl.ds(m * SLICE, SLICE)], rows_ref)
    for h in range(GROUPS):
        w_load(h)
    late = (keep(q_hbm, q_ref), keep(g_hbm, g_ref))
    holders = [jnp.clip(source_of(d, n)[0], 0, N_DP - 1) for n in range(DSEQ)]
    rows_copy.wait()
    fill()
    pl.semaphore_wait(barrier, len(peers))
    rows_out(0)
    rows_out(1)
    rows_out(2)
    rows_out(3)
    w_begin(0)
    w_begin(1)
    w_first(0)
    rows_out(4)
    rows_out(5)
    stage1(0)
    stage1(1)
    stage2(0)
    stage1(2)
    stage2(1)
    stage3(0)
    stage1(3)
    stage2(2)
    rows_in(0)
    w_step(0, 1)
    rows_out(6)
    rows_out(7)
    stage3(1)
    stage2(3)
    rows_in(1)
    stage1(4)
    stage3(2)
    stage3(3)
    stage1(5)
    stage2(4)
    rows_in(2)
    w_step(0, 2)
    w_first(1)
    rows_in(3)
    stage2(5)
    stage3(4)
    stage1(6)
    rows_in(4)
    stage3(5)
    stage1(7)
    stage2(6)
    w_step(0, 3)
    rows_in(5)
    stage2(7)
    w_step(1, 1)
    w_side(0, 3)
    w_last(0)
    stage3(6)
    w_side(0, -3)
    stage3(7)
    w_side(0, 4)
    w_step(1, 2)
    w_in(0)
    rows_in(7)
    project_range(0, 0, 4)
    project_range(0, 7, 8)
    rows_in(6)
    project_range(0, 4, 7)
    for copy in late:
        copy.wait()
    attend_range(0, 0, 2)
    attend_range(0, 2, 4)
    attend_range(0, 4, 6)
    w_step(1, 3)
    attend_range(0, 6, 8)
    blocks(0)
    w_last(1)
    w_in(1)
    project_range(1, 0, 4)
    project_range(1, 4, 8)
    attend_range(1, 0, 2)
    chain3(0)
    attend_range(1, 2, 4)
    attend_range(1, 4, 6)
    attend_range(1, 6, 8)
    blocks(1)
    chain2(0)
    partner(0)
    chain3(1)
    chain1(0)
    chain2(1)
    partner(1)
    chain0(0)
    chain1(1)
    chain0(1)
    for copy in sent:
        copy.wait_send()
    for h in range(GROUPS):
        drain(h)


def hand_over(*refs):
    for i in range(3):
        refs[3 + i][...] = refs[i][...]


def per_device(encoder_rows, w_key, w_value, query, grad_context, source):
    rows, inner = w_key.shape
    vmem = pl.BlockSpec(memory_space=pltpu.VMEM)
    hbm = pl.BlockSpec(memory_space=pl.ANY)
    dma = pltpu.SemaphoreType.DMA
    wide = 2 * GW
    outs = pl.pallas_call(
        kernel,
        out_shape=(
            jax.ShapeDtypeStruct(query.shape, BF16),
            jax.ShapeDtypeStruct(query.shape, BF16),
            jax.ShapeDtypeStruct((2, rows, inner), F32),
        ),
        in_specs=[pl.BlockSpec(memory_space=pltpu.SMEM), hbm, hbm, hbm, hbm, hbm],
        out_specs=(vmem, vmem, vmem),
        scratch_shapes=[pltpu.VMEM((N_DP, CROWS, SLICE), BF16)] * CHUNKS
        + [pltpu.VMEM((DSEQ * CROWS, SLICE), BF16)] * CHUNKS
        + [
            pltpu.VMEM((N_DP - 1, CHUNKS, CROWS, SLICE), BF16),
            pltpu.VMEM((EX_DEV, SEQ, SLICE), BF16),
            pltpu.VMEM(query.shape, BF16),
            pltpu.VMEM(query.shape, BF16),
            pltpu.VMEM((N_MP, CHUNKS, DSEQ * CROWS, SLICE), BF16),
            pltpu.VMEM((GROUPS, 2, N_DP, 2, rows, wide), BF16),
            pltpu.VMEM((GROUPS, CHUNKS, DSEQ, CROWS, wide), BF16),
            pltpu.VMEM((GROUPS, CHUNKS, DSEQ, CROWS, wide), BF16),
            pltpu.VMEM((GROUPS, 8, 2 * rows, wide), BF16),
            pltpu.VMEM((GROUPS, 8, 2 * rows, wide), BF16),
            pltpu.VMEM((GROUPS, 8, 2 * rows, wide), F32),
            pltpu.VMEM((GROUPS, 4, rows, wide), BF16),
            pltpu.VMEM((GROUPS, 4, rows, wide), BF16),
            pltpu.VMEM((GROUPS, 4, rows, wide), BF16),
            pltpu.VMEM((GROUPS, 4, rows, wide), BF16),
            pltpu.VMEM((GROUPS, 8, rows, wide), BF16),
            pltpu.VMEM((GROUPS, 8, rows, wide), BF16),
            dma((GATHER_COPIES,)), dma((GATHER_COPIES,)), dma((3 + 2 * GROUPS + CHUNKS,)),
            dma((GROUPS, 8)), dma((GROUPS, 8)), dma((GROUPS, 4)), dma((GROUPS, 4)),
            dma((GROUPS, 4)), dma((GROUPS, 4)), dma((GROUPS, 8)), dma((GROUPS, 8)),
        ],
        compiler_params=pltpu.CompilerParams(
            collective_id=0, has_side_effects=True, vmem_limit_bytes=61 * 2**20
        ),
        name="cross_attention",
    )(source, encoder_rows, w_key, w_value, query, grad_context)
    return pl.pallas_call(
        hand_over,
        out_shape=tuple(jax.ShapeDtypeStruct(o.shape, o.dtype) for o in outs),
        in_specs=[vmem] * 3,
        out_specs=(vmem,) * 3,
        name="hand_over",
    )(*outs)


def solution(mesh):
    return jax.shard_map(
        per_device,
        mesh=mesh,
        in_specs=(
            P(("section", "dp"), None, None),
            P(("section", "dp"), "mp"),
            P(("section", "dp"), "mp"),
            P(("section", "dp"), None, "mp"),
            P(("section", "dp"), None, "mp"),
            P(),
        ),
        out_specs=(
            P(("section", "dp"), None, "mp"),
            P(("section", "dp"), None, "mp"),
            P(None, ("section", "dp"), "mp"),
        ),
        check_vma=False,
    )
```

```python
import jax
import jax.numpy as jnp
from jax import lax
from jax.experimental import pallas as pl
from jax.experimental.pallas import tpu as pltpu
from jax.sharding import PartitionSpec as P

HEAD_DIM = 64
MESH = pl.DeviceIdType.MESH
BF16 = jnp.bfloat16
F32 = jnp.float32
N_DP = 8
N_MP = 8
DSEQ = 4
SEQ = 256
CHUNKS = 8
CROWS = SEQ // CHUNKS
SLICE = 512
WROWS = 128
LANES = 128
EX_DEV = 3
GROUPS = 2
GW = SLICE // GROUPS
PAIRS = GW // LANES
ON_Z = (2, 3,)
ORDER = (4, 3, 5, 2, 6, 1, 7)
LIGHT = (7,)
GATHER_COPIES = 15 * CHUNKS + 2 * len(LIGHT) + 27 * GROUPS


def nt(a, b):
    return lax.dot_general(a, b, (((1,), (1,)), ((), ())), preferred_element_type=F32)


def nn(a, b):
    return lax.dot_general(a, b, (((1,), (0,)), ((), ())), preferred_element_type=F32)


def tn(a, b):
    return lax.dot_general(a, b, (((0,), (0,)), ((), ())), preferred_element_type=F32)


def attend_pair(k, v, q, g):
    rows = q.shape[0]
    low = lax.broadcasted_iota(jnp.int32, q.shape, 1) < HEAD_DIM
    zero = jnp.zeros_like(q)
    q2 = jnp.concatenate([jnp.where(low, q, zero), jnp.where(low, zero, q)], axis=0)
    g2 = jnp.concatenate([jnp.where(low, g, zero), jnp.where(low, zero, g)], axis=0)
    scores = nt(k, q2)
    expo = jnp.exp(scores - jnp.max(scores, axis=0, keepdims=True))
    weights = expo * (1.0 / jnp.sum(expo, axis=0, keepdims=True))
    probs = weights.astype(BF16)
    dprobs = nt(v, g2)
    delta = jnp.sum(weights * dprobs, axis=0, keepdims=True)
    grads = (weights * (dprobs - delta)).astype(BF16)
    ctx = tn(probs, v)
    gq = tn(grads, k)
    return (
        jnp.where(low, ctx[:rows], ctx[rows:]).astype(BF16),
        jnp.where(low, gq[:rows], gq[rows:]).astype(BF16),
        nn(grads, q2).astype(BF16),
        nn(probs, g2).astype(BF16),
    )


def kernel(src_ref, e_hbm, wk_hbm, wv_hbm, q_hbm, g_hbm, ctx_ref, gq_ref, o_ref, *scratch):
    slots, picks = scratch[0:CHUNKS], scratch[CHUNKS : 2 * CHUNKS]
    (snd, rows_ref, q_ref, g_ref, ef, wf, kv, terms, tosib, fromsib, own, ysend, yrecv, psend,
     precv, zsend, zrecv, ssem, rsem, lsem, sib_s, sib_r, y_s, y_r, p_s, p_r, z_s, z_r) = scratch[
        2 * CHUNKS :
    ]
    s, d, m = lax.axis_index("section"), lax.axis_index("dp"), lax.axis_index("mp")
    core, ylo = s % 2, s // 2
    sib, ypart = (s ^ 1, d, m), (s ^ 2, d, m)
    zr, zl = (s, (d + 1) % 8, m), (s, (d + 7) % 8, m)
    x, yhi = m % 4, m // 4
    m_r, m_l, m_2 = yhi * 4 + (x + 1) % 4, yhi * 4 + (x + 3) % 4, yhi * 4 + (x + 2) % 4
    xr, xl, y2 = (s, d, m_r), (s, d, m_l), (s, d, m ^ 4)

    barrier = pltpu.get_barrier_semaphore()
    peers = [sib, ypart, xr, xl, y2] + [(s, (d + k) % 8, m) for k in range(1, 8)]
    for peer in peers:
        pl.semaphore_signal(barrier, inc=1, device_id=peer, device_id_type=MESH)

    sent, local = [], []

    def put(src, dst, to):
        i = len(sent)
        copy = pltpu.make_async_remote_copy(
            src_ref=src, dst_ref=dst, send_sem=ssem.at[i], recv_sem=rsem.at[i],
            device_id=to, device_id_type=MESH,
        )
        copy.start()
        sent.append(copy)
        return copy

    def keep(src, dst):
        copy = pltpu.make_async_copy(src, dst, lsem.at[len(local)])
        copy.start()
        local.append(copy)
        return copy

    arrive, own_pick = [None] * CHUNKS, [None] * CHUNKS
    first, second, third = [None] * CHUNKS, [None] * CHUNKS, [None] * CHUNKS
    mid = DSEQ * CROWS // 2

    def source_of(reader, n):
        at = src_ref[s * (N_DP * DSEQ) + reader * DSEQ + n]
        return lax.div(at, jnp.int32(EX_DEV)) - s * N_DP, lax.rem(at, jnp.int32(EX_DEV))

    def example_for(reader):
        chosen = jnp.int32(0)
        for n in range(DSEQ):
            holder, example = source_of(reader, n)
            chosen = chosen + jnp.where(holder == d, example, 0)
        return chosen

    def fill():
        for k in range(N_DP):
            chosen = example_for((d + k) % 8)
            for c in range(CHUNKS):
                part = rows_ref[chosen, c * CROWS : (c + 1) * CROWS, :]
                if k:
                    snd[k - 1, c] = part
                else:
                    slots[c][d] = part

    def rows_out(c):
        arrive[c] = [put(snd.at[k - 1, c], slots[c].at[d], (s, (d + k) % 8, m)) for k in ORDER]

    def stage1(c):
        for copy in arrive[c]:
            copy.wait_recv()
        for n in range(DSEQ):
            picks[c][pl.ds(n * CROWS, CROWS), :] = slots[c][holders[n]]
        mine = ef.at[m, c]
        first[c] = (put(picks[c], mine, xr), put(picks[c], mine, xl), put(picks[c], mine, y2))
        own_pick[c] = keep(picks[c], mine)

    def stage2(c):
        to_r, to_l, to_y = first[c]
        to_y.wait_recv()
        part = ef.at[m ^ 4, c]
        out_r, out_l = put(part, part, xr), put(part, part, xl)
        to_r.wait_recv()
        lo = ef.at[m_l, c, pl.ds(0, mid)]
        a = put(lo, lo, xr)
        to_l.wait_recv()
        hi = ef.at[m_r, c, pl.ds(mid, mid)]
        b = put(hi, hi, xl)
        second[c] = (a, b, out_r, out_l)

    def stage3(c):
        if c in LIGHT:
            a, b, out_r, out_l = second[c]
            out_r.wait_recv()
            lo = ef.at[m_l ^ 4, c, pl.ds(0, mid)]
            far_a = put(lo, lo, xr)
            out_l.wait_recv()
            hi = ef.at[m_r ^ 4, c, pl.ds(mid, mid)]
            far_b = put(hi, hi, xl)
            third[c] = (a, b, far_a, far_b)
        else:
            second[c][0].wait_recv()
            second[c][1].wait_recv()
            far = ef.at[m_2, c]
            third[c] = (second[c][2], second[c][3], put(far, far, y2))

    def rows_in(c):
        for copy in third[c]:
            copy.wait_recv()
        own_pick[c].wait()

    w_y, w_own = [None] * GROUPS, [None] * GROUPS
    wz = [{} for h in range(GROUPS)]
    from_sib = [[] for h in range(GROUPS)]
    w_yrecv = [{} for h in range(GROUPS)]

    def wpair(h, k):
        return wf.at[h, core, (d + k + 8) % 8]

    def w_load(h):
        at = pl.ds(h * GW, GW)
        mine = wf.at[h, core, d, ylo]
        w_own[h] = (
            keep(wk_hbm.at[:, at], mine.at[:, pl.ds(0, GW)]),
            keep(wv_hbm.at[:, at], mine.at[:, pl.ds(GW, GW)]),
        )

    def w_begin(h):
        for copy in w_own[h]:
            copy.wait()
        mine = wf.at[h, core, d, ylo]
        w_y[h] = put(mine, mine, ypart)

    def w_first(h):
        w_y[h].wait_recv()
        both = wpair(h, 0)
        wz[h][1] = put(both, both, zr)
        wz[h][-1] = put(both, both, zl)
        from_sib[h].append(put(both, both, sib))

    def w_next(h, j, blk, row, rows, to):
        if j + 1 <= ON_Z[h]:
            return put(blk, blk, to)
        one = blk.at[row] if j < 3 or ON_Z[h] == 3 else blk.at[ylo, rows]
        return put(one, one, to)

    def w_step(h, j):
        half_rows = WROWS // 2
        wz[h][j].wait_recv()
        right = wpair(h, -j)
        wz[h][j + 1] = w_next(h, j, right, ylo, pl.ds(0, half_rows), zr)
        wz[h][-j].wait_recv()
        left = wpair(h, j)
        row = 1 - ylo if j == 3 and ON_Z[h] == 3 else ylo
        wz[h][-j - 1] = w_next(h, j, left, row, pl.ds(half_rows, half_rows), zl)
        for k, blk in ((j, right), (-j, left)):
            if j > ON_Z[h]:
                one = blk.at[ylo]
                w_yrecv[h][k] = put(one, one, ypart)
                blk = one
            from_sib[h].append(put(blk, blk, sib))

    def w_last(h):
        wz[h][4].wait_recv()
        wz[h][-4].wait_recv()
        far = wpair(h, 4)
        if ON_Z[h] < 3:
            far = far.at[ylo]
            w_yrecv[h][4] = put(far, far, ypart)
        from_sib[h].append(put(far, far, sib))

    def w_side(h, k):
        w_yrecv[h][k].wait_recv()
        blk = wpair(h, -k).at[1 - ylo]
        from_sib[h].append(put(blk, blk, sib))

    def w_in(h):
        for copy in from_sib[h]:
            copy.wait_recv()

    def weight_rows(h, i):
        yy, cc, z0 = i // 4, (i // 2) % 2, (i % 2) * 4
        return [wf[h, cc, z0 + k, yy] for k in range(4)]

    def project_range(h, lo, hi):
        rows = (hi - lo) * DSEQ * CROWS
        lhs = jnp.concatenate([ef[i, lo:hi].reshape(rows, SLICE) for i in range(N_MP)], axis=1)
        rhs = jnp.concatenate([r for i in range(N_MP) for r in weight_rows(h, i)], axis=0)
        kv[h, lo:hi] = nn(lhs, rhs).astype(BF16).reshape(hi - lo, DSEQ, CROWS, 2 * GW)

    def attend_range(h, lo, hi):
        def body(t, carry):
            n, p = t // PAIRS, t % PAIRS
            at_k = pl.ds(pl.multiple_of(p * LANES, LANES), LANES)
            at_v = pl.ds(pl.multiple_of(p * LANES + GW, LANES), LANES)
            at_q = pl.ds(pl.multiple_of(p * LANES + h * GW, LANES), LANES)
            k = kv[h, :, n, :, at_k].reshape(SEQ, LANES)
            v = kv[h, :, n, :, at_v].reshape(SEQ, LANES)
            ctx, gq, kt, vt = attend_pair(k, v, q_ref[n, :, at_q], g_ref[n, :, at_q])
            ctx_ref[n, :, at_q] = ctx
            gq_ref[n, :, at_q] = gq
            terms[h, :, n, :, at_k] = kt.reshape(CHUNKS, CROWS, LANES)
            terms[h, :, n, :, at_v] = vt.reshape(CHUNKS, CROWS, LANES)
            return carry

        lax.fori_loop(lo, hi, body, 0)

    def remote(src, dst, ss, rs, to):
        return pltpu.make_async_remote_copy(
            src_ref=src, dst_ref=dst, send_sem=ss, recv_sem=rs, device_id=to, device_id_type=MESH
        )

    def to_sib(h, i):
        return remote(tosib.at[h, i], fromsib.at[h, i], sib_s.at[h, i], sib_r.at[h, i], sib)

    def to_y(h, k):
        return remote(ysend.at[h, k], yrecv.at[h, k], y_s.at[h, k], y_r.at[h, k], ypart)

    def to_p(h, k):
        to = zr if k % 2 == 0 else zl
        return remote(psend.at[h, k], precv.at[h, k], p_s.at[h, k], p_r.at[h, k], to)

    half = WROWS // 2

    def to_z(h, k, r):
        to = zr if k % 2 == 0 else zl
        rows = pl.ds(r * half, half)
        return remote(
            zsend.at[h, k, rows], zrecv.at[h, k, rows], z_s.at[h, k, r], z_r.at[h, k, r], to
        )

    def z_rows(k, i):
        r = (1, 0)[i] if k == 0 else i
        return r, slice(r * half, (r + 1) * half), slice(WROWS + r * half, WROWS + (r + 1) * half)

    def columns(yy, cc, dd):
        block = (yy * 2 + cc) * 8 + dd
        at = pl.ds(pl.multiple_of((block % 4) * WROWS, WROWS), WROWS)
        return ef[block // 4, :, :, at].reshape(DSEQ * SEQ, WROWS)

    def block_pair(h, cc, dd):
        e = jnp.concatenate([columns(1 - ylo, cc, dd), columns(ylo, cc, dd)], axis=1)
        return tn(e, terms[h].reshape(DSEQ * SEQ, 2 * GW))

    def absorb(h, k):
        to_sib(h, k).wait_recv()
        own[h, k] += fromsib[h, k].astype(F32)

    def chain4(h):
        to_y(h, 0).wait_recv()
        total = own[h, 0, WROWS:] + yrecv[h, 0].astype(F32)
        zsend[h, 0, :half] = total[:half].astype(BF16)
        to_z(h, 0, 0).start()
        zsend[h, 1, half:] = total[half:].astype(BF16)
        to_z(h, 1, 1).start()

    def blocks(h):
        def step(i, carry):
            j = (i % 2) * (4 - (i + 1) // 2) + (1 - i % 2) * (4 + i // 2)
            dd = (d + j) % 8
            tosib[h, i] = block_pair(h, 1 - core, dd).astype(BF16)
            to_sib(h, i).start()
            own[h, i] = block_pair(h, core, dd)

            @pl.when(i == 6)
            def _():
                chain4(h)

            @pl.when(i > 0)
            def _():
                absorb(h, i - 1)

            @pl.when((i > 0) & (i < 4))
            def _():
                ysend[h, i - 1] = own[h, i - 1, :WROWS].astype(BF16)
                to_y(h, i - 1).start()

            for k in range(2):

                @pl.when(i == 4 + k)
                def _(k=k):
                    psend[h, k] = own[h, 3 + k, :WROWS].astype(BF16)
                    to_p(h, k).start()

            return carry

        lax.fori_loop(0, 8, step, 0)
        absorb(h, 7)

    def chain3(h):
        for k in range(2):
            to_y(h, 1 + k).wait_recv()
            for i in range(2):
                r, rows, mine = z_rows(k, i)
                part = own[h, 1 + k, mine] + yrecv[h, 1 + k, rows].astype(F32)
                if r == k:
                    to_z(h, k, k).wait_recv()
                    part = part + zrecv[h, k, rows].astype(F32)
                zsend[h, 2 + k, rows] = part.astype(BF16)
                to_z(h, 2 + k, r).start()
        for k in range(2):
            to_p(h, k).wait_recv()
            psend[h, 2 + k] = (own[h, 5 + k, :WROWS] + precv[h, k].astype(F32)).astype(BF16)
            to_p(h, 2 + k).start()

    def chain_step(h, j):
        at = 2 * (3 - j)
        for i in range(2):
            for k in range(2):
                r, rows, mine = z_rows(k, i)
                to_z(h, at + k, r).wait_recv()
                part = own[h, at + 1 + k, mine] + zrecv[h, at + k, rows].astype(F32)
                zsend[h, at + 2 + k, rows] = part.astype(BF16)
                to_z(h, at + 2 + k, r).start()

    def chain2(h):
        chain_step(h, 2)

    def partner(h):
        total = own[h, 7, :WROWS]
        for k in range(2):
            to_p(h, 2 + k).wait_recv()
            total = total + precv[h, 2 + k].astype(F32)
        ysend[h, 3] = total.astype(BF16)
        to_y(h, 3).start()

    def chain1(h):
        chain_step(h, 1)

    def chain0(h):
        total = own[h, 7, WROWS:]
        for k in range(2):
            for r in range(2):
                to_z(h, 6 + k, r).wait_recv()
            total = total + zrecv[h, 6 + k].astype(F32)
        to_y(h, 3).wait_recv()
        total = total + yrecv[h, 3].astype(F32)
        at = pl.ds(h * GW, GW)
        o_ref[0, :, at] = total[:, :GW]
        o_ref[1, :, at] = total[:, GW:]

    def drain(h):
        for k in range(8):
            to_sib(h, k).wait_send()
            for r in (k,) if k < 2 else range(2):
                to_z(h, k, r).wait_send()
        for k in range(4):
            to_y(h, k).wait_send()
            to_p(h, k).wait_send()

    rows_copy = keep(e_hbm.at[:, :, pl.ds(m * SLICE, SLICE)], rows_ref)
    for h in range(GROUPS):
        w_load(h)
    late = (keep(q_hbm, q_ref), keep(g_hbm, g_ref))
    holders = [jnp.clip(source_of(d, n)[0], 0, N_DP - 1) for n in range(DSEQ)]
    rows_copy.wait()
    fill()
    pl.semaphore_wait(barrier, len(peers))
    rows_out(0)
    rows_out(1)
    rows_out(2)
    rows_out(3)
    w_begin(0)
    w_begin(1)
    w_first(0)
    rows_out(4)
    rows_out(5)
    stage1(0)
    stage1(1)
    stage2(0)
    stage1(2)
    stage2(1)
    stage3(0)
    stage1(3)
    stage2(2)
    rows_in(0)
    w_step(0, 1)
    rows_out(6)
    rows_out(7)
    stage3(1)
    stage2(3)
    rows_in(1)
    stage1(4)
    stage3(2)
    stage3(3)
    stage1(5)
    stage2(4)
    rows_in(2)
    w_step(0, 2)
    w_first(1)
    rows_in(3)
    stage2(5)
    stage3(4)
    stage1(6)
    rows_in(4)
    stage3(5)
    stage1(7)
    stage2(6)
    w_step(0, 3)
    rows_in(5)
    stage2(7)
    w_step(1, 1)
    w_side(0, 3)
    w_last(0)
    stage3(6)
    w_side(0, -3)
    stage3(7)
    w_side(0, 4)
    w_step(1, 2)
    w_in(0)
    rows_in(7)
    project_range(0, 0, 4)
    project_range(0, 7, 8)
    rows_in(6)
    project_range(0, 4, 7)
    for copy in late:
        copy.wait()
    attend_range(0, 0, 2)
    attend_range(0, 2, 4)
    attend_range(0, 4, 6)
    w_step(1, 3)
    attend_range(0, 6, 8)
    blocks(0)
    w_last(1)
    w_in(1)
    project_range(1, 0, 4)
    project_range(1, 4, 8)
    attend_range(1, 0, 2)
    chain3(0)
    attend_range(1, 2, 4)
    attend_range(1, 4, 6)
    attend_range(1, 6, 8)
    blocks(1)
    chain2(0)
    partner(0)
    chain3(1)
    chain1(0)
    chain2(1)
    partner(1)
    chain0(0)
    chain1(1)
    chain0(1)
    for copy in sent:
        copy.wait_send()
    for h in range(GROUPS):
        drain(h)


def hand_over(*refs):
    for i in range(3):
        refs[3 + i][...] = refs[i][...]


def per_device(encoder_rows, w_key, w_value, query, grad_context, source):
    rows, inner = w_key.shape
    vmem = pl.BlockSpec(memory_space=pltpu.VMEM)
    hbm = pl.BlockSpec(memory_space=pl.ANY)
    dma = pltpu.SemaphoreType.DMA
    wide = 2 * GW
    outs = pl.pallas_call(
        kernel,
        out_shape=(
            jax.ShapeDtypeStruct(query.shape, BF16),
            jax.ShapeDtypeStruct(query.shape, BF16),
            jax.ShapeDtypeStruct((2, rows, inner), F32),
        ),
        in_specs=[pl.BlockSpec(memory_space=pltpu.SMEM), hbm, hbm, hbm, hbm, hbm],
        out_specs=(vmem, vmem, vmem),
        scratch_shapes=[pltpu.VMEM((N_DP, CROWS, SLICE), BF16)] * CHUNKS
        + [pltpu.VMEM((DSEQ * CROWS, SLICE), BF16)] * CHUNKS
        + [
            pltpu.VMEM((N_DP - 1, CHUNKS, CROWS, SLICE), BF16),
            pltpu.VMEM((EX_DEV, SEQ, SLICE), BF16),
            pltpu.VMEM(query.shape, BF16),
            pltpu.VMEM(query.shape, BF16),
            pltpu.VMEM((N_MP, CHUNKS, DSEQ * CROWS, SLICE), BF16),
            pltpu.VMEM((GROUPS, 2, N_DP, 2, rows, wide), BF16),
            pltpu.VMEM((GROUPS, CHUNKS, DSEQ, CROWS, wide), BF16),
            pltpu.VMEM((GROUPS, CHUNKS, DSEQ, CROWS, wide), BF16),
            pltpu.VMEM((GROUPS, 8, 2 * rows, wide), BF16),
            pltpu.VMEM((GROUPS, 8, 2 * rows, wide), BF16),
            pltpu.VMEM((GROUPS, 8, 2 * rows, wide), F32),
            pltpu.VMEM((GROUPS, 4, rows, wide), BF16),
            pltpu.VMEM((GROUPS, 4, rows, wide), BF16),
            pltpu.VMEM((GROUPS, 4, rows, wide), BF16),
            pltpu.VMEM((GROUPS, 4, rows, wide), BF16),
            pltpu.VMEM((GROUPS, 8, rows, wide), BF16),
            pltpu.VMEM((GROUPS, 8, rows, wide), BF16),
            dma((GATHER_COPIES,)), dma((GATHER_COPIES,)), dma((3 + 2 * GROUPS + CHUNKS,)),
            dma((GROUPS, 8)), dma((GROUPS, 8)), dma((GROUPS, 4)), dma((GROUPS, 4)),
            dma((GROUPS, 4)), dma((GROUPS, 4)), dma((GROUPS, 8, 2)), dma((GROUPS, 8, 2)),
        ],
        compiler_params=pltpu.CompilerParams(
            collective_id=0, has_side_effects=True, vmem_limit_bytes=61 * 2**20
        ),
        name="cross_attention",
    )(source, encoder_rows, w_key, w_value, query, grad_context)
    return pl.pallas_call(
        hand_over,
        out_shape=tuple(jax.ShapeDtypeStruct(o.shape, o.dtype) for o in outs),
        in_specs=[vmem] * 3,
        out_specs=(vmem,) * 3,
        name="hand_over",
    )(*outs)


def solution(mesh):
    return jax.shard_map(
        per_device,
        mesh=mesh,
        in_specs=(
            P(("section", "dp"), None, None),
            P(("section", "dp"), "mp"),
            P(("section", "dp"), "mp"),
            P(("section", "dp"), None, "mp"),
            P(("section", "dp"), None, "mp"),
            P(),
        ),
        out_specs=(
            P(("section", "dp"), None, "mp"),
            P(("section", "dp"), None, "mp"),
            P(None, ("section", "dp"), "mp"),
        ),
        check_vma=False,
    )
```
